32 devices in a mesh: dp: 8 (over y, x, core), dap: 4 (over z).
Axes of the slice: x: 2, y: 2, z: 4, core: 2. Of those that a mesh axis runs over, the one named last changes fastest.
Arguments:
- pair_act: bfloat16 [8, 128, 128, 128], P('dp', 'dap'), may hold values from -6 to 6
- pair_cot: bfloat16 [8, 128, 128, 128], P('dp', 'dap'), may hold values from -6 to 6
- in_gain: float32 [128], replicated, may hold values from 0.25 to 1.75
- in_bias: float32 [128], replicated, may hold values from -3 to 3
- proj_weight: bfloat16 [128, 512], replicated, may hold values from -0.5 to 0.5
- gate_weight: bfloat16 [128, 128], replicated, may hold values from -0.5 to 0.5
- out_gain: float32 [128], replicated, may hold values from 0.25 to 1.75
- out_bias: float32 [128], replicated, may hold values from -3 to 3
- out_weight: bfloat16 [128, 128], replicated, may hold values from -0.5 to 0.5
Outputs:
- update: bfloat16 [8, 128, 128, 128], P('dp', 'dap')
- pair_grad: bfloat16 [8, 128, 128, 128], P('dp', 'dap')
- proj_grad: float32 [128, 512], replicated
- gate_grad: float32 [128, 128], replicated
- out_grad: float32 [128, 128], replicated
- in_norm_grad: float32 [2, 128], replicated
- out_norm_grad: float32 [2, 128], replicated
The draws below stay inside these ranges and needn't reach their ends.
All inputs are finite; a program needn't handle non-finite values.
Results may differ from the reference program's by a relative error of at most 0.0084.
Values may be sent and summed in bfloat16 or wider, within the bound.
A program may use at most 64 MiB of HBM per device.

```python
import jax
import jax.numpy as jnp
from jax import lax

C = 128
CH = 128
N = 128
CROPS = 8


def shard_levels(key, shape, cuts, smallest, high):
    def one(position, shards_of):
        draws = jax.random.uniform(jax.random.fold_in(jax.random.fold_in(key, 6), position), (shards_of,), jnp.float32, smallest / len(cuts), high / len(cuts))
        return jnp.repeat(jnp.exp(draws), shape[position] // shards_of).reshape((-1,) + (1,) * (len(shape) - position - 1))

    loudness = one(*cuts[0])
    for cut in cuts[1:]:
        loudness = loudness * one(*cut)
    return loudness


def scatter_about(key, shape, deviation, reach, shards=(), dtype=jnp.bfloat16):
    drawn = jax.random.normal(key, shape, jnp.float32) * deviation
    if len(shards) > 0:
        drawn = shard_levels(key, shape, shards, -0.22, 0.18) * drawn
    return jnp.clip(drawn, min=-reach, max=reach).astype(dtype)


def setup_inputs(seed: int = 0) -> dict:
    key_of = jax.random.split(jax.random.key(seed), 10)
    pair_act = scatter_about(key_of[0], (CROPS, N, N, C), 1.0, 6.0, ((0, 8), (1, 4)))
    pair_cot = scatter_about(key_of[1], (CROPS, N, N, C), 1.0, 6.0, ((0, 8), (1, 4)))
    in_gain = jnp.clip(1.0 + 0.15 * jax.random.normal(key_of[2], (C,), jnp.float32), 0.25, 1.75)
    in_bias = scatter_about(key_of[3], (C,), 0.3, 3.0, (), jnp.float32)
    proj_weight = scatter_about(key_of[4], (C, 4 * CH), C ** -0.5, 0.5)
    gate_weight = scatter_about(key_of[5], (C, C), C ** -0.5, 0.5)
    out_gain = jnp.clip(1.0 + 0.15 * jax.random.normal(key_of[6], (CH,), jnp.float32), 0.25, 1.75)
    out_bias = scatter_about(key_of[7], (CH,), 0.3, 3.0, (), jnp.float32)
    out_weight = scatter_about(key_of[8], (CH, C), CH ** -0.5, 0.5)
    return dict(pair_act=pair_act, pair_cot=pair_cot, in_gain=in_gain, in_bias=in_bias, proj_weight=proj_weight, gate_weight=gate_weight, out_gain=out_gain, out_bias=out_bias, out_weight=out_weight)


epsilon = 1e-05

def norm_rows(values, along):
    row_mean = lax.optimization_barrier(jnp.mean(values, axis=along, keepdims=True))
    centred = values - row_mean
    row_var = lax.optimization_barrier(jnp.mean(centred * centred, axis=along, keepdims=True))
    inv_std = lax.rsqrt(row_var + epsilon)
    return (centred * inv_std, inv_std)

def norm_back(grad_hat, x_hat, inv_std, along):
    first = lax.optimization_barrier(jnp.mean(grad_hat, axis=along, keepdims=True))
    second = lax.optimization_barrier(jnp.mean(grad_hat * x_hat, axis=along, keepdims=True))
    return (grad_hat - first - x_hat * second) * inv_std

def reference(pair_act, pair_cot, in_gain, in_bias, proj_weight, gate_weight, out_gain, out_bias, out_weight):
    f32 = jnp.float32
    bf16 = jnp.bfloat16

    def one_crop(operands):
        pair_one, cot_one = operands
        flat_act = pair_one.reshape(N * N, C).astype(f32)
        in_hat, in_inv = norm_rows(flat_act, 1)
        normed = (in_hat * in_gain + in_bias).astype(bf16)
        projected = jnp.dot(normed, proj_weight, preferred_element_type=f32)
        pre_ag = projected[:, 0:CH]
        pre_ap = projected[:, CH:2 * CH]
        pre_bg = projected[:, 2 * CH:3 * CH]
        pre_bp = projected[:, 3 * CH:4 * CH]
        sig_a = jax.nn.sigmoid(pre_ag)
        sig_b = jax.nn.sigmoid(pre_bg)
        left_act = (sig_a * pre_ap).astype(bf16).reshape(N, N, CH)
        right_act = (sig_b * pre_bp).astype(bf16).reshape(N, N, CH)
        tri_out = jnp.einsum('ikh,jkh->ijh', left_act.astype(f32), right_act.astype(f32)).astype(bf16)
        tri_hat, tri_inv = norm_rows(tri_out.reshape(N * N, CH).astype(f32), 1)
        tri_norm = (tri_hat * out_gain + out_bias).astype(bf16)
        gate_val = jax.nn.sigmoid(jnp.dot(normed, gate_weight, preferred_element_type=f32))
        mixed = jnp.dot(tri_norm, out_weight, preferred_element_type=f32)
        update = (gate_val * mixed).astype(bf16)
        cot_flat = cot_one.reshape(N * N, C).astype(f32)
        d_mixed = (cot_flat * gate_val).astype(bf16)
        d_gate = (cot_flat * mixed * gate_val * (1.0 - gate_val)).astype(bf16)
        out_part = jnp.dot(tri_norm.T, d_mixed, preferred_element_type=f32)
        gate_part = jnp.dot(normed.T, d_gate, preferred_element_type=f32)
        d_norm_out = jnp.dot(d_mixed, out_weight.T, preferred_element_type=f32)
        out_norm_part = jnp.stack([lax.optimization_barrier(jnp.sum(d_norm_out * tri_hat, axis=0)), lax.optimization_barrier(jnp.sum(d_norm_out, axis=0))])
        d_tri = norm_back(d_norm_out * out_gain, tri_hat, tri_inv, 1).astype(bf16).reshape(N, N, CH)
        d_left = jnp.einsum('ijh,jkh->ikh', d_tri.astype(f32), right_act.astype(f32)).astype(bf16)
        d_right = jnp.einsum('ijh,ikh->jkh', d_tri.astype(f32), left_act.astype(f32)).astype(bf16)
        left_grad = d_left.reshape(N * N, CH).astype(f32)
        right_grad = d_right.reshape(N * N, CH).astype(f32)
        d_proj = jnp.concatenate([left_grad * pre_ap * sig_a * (1.0 - sig_a), left_grad * sig_a, right_grad * pre_bp * sig_b * (1.0 - sig_b), right_grad * sig_b], axis=1).astype(bf16)
        proj_part = jnp.dot(normed.T, d_proj, preferred_element_type=f32)
        d_normed = jnp.dot(d_proj, proj_weight.T, preferred_element_type=f32) + jnp.dot(d_gate, gate_weight.T, preferred_element_type=f32)
        in_norm_part = jnp.stack([lax.optimization_barrier(jnp.sum(d_normed * in_hat, axis=0)), lax.optimization_barrier(jnp.sum(d_normed, axis=0))])
        pair_grad = norm_back(d_normed * in_gain, in_hat, in_inv, 1).astype(bf16)
        return (update.reshape(N, N, C), pair_grad.reshape(N, N, C), proj_part, gate_part, out_part, in_norm_part, out_norm_part)
    results = lax.map(one_crop, (pair_act, pair_cot))
    update, pair_grad, proj_all, gate_all, out_all, in_all, outn_all = results
    scale = 1.0 / N
    return (update, pair_grad, lax.optimization_barrier(jnp.sum(proj_all, axis=0)) * scale, lax.optimization_barrier(jnp.sum(gate_all, axis=0)) * scale, lax.optimization_barrier(jnp.sum(out_all, axis=0)) * scale, lax.optimization_barrier(jnp.sum(in_all, axis=0)) * scale, lax.optimization_barrier(jnp.sum(outn_all, axis=0)) * scale)
```

```python
import functools

import jax
import jax.numpy as jnp
from jax import lax
from jax.experimental import pallas as pl
from jax.experimental.pallas import tpu as pltpu
from jax.sharding import PartitionSpec as P

epsilon = 1e-05
f32 = jnp.float32
bf16 = jnp.bfloat16
STEP = 8
CUT = 16


def mm(a, b):
    return jnp.dot(a, b, preferred_element_type=f32)


def mm_t(a, b):
    return lax.dot_general(a, b, (((1,), (1,)), ((), ())), preferred_element_type=f32)


def sigmoid(v):
    return 0.5 * jnp.tanh(0.5 * v) + 0.5


def norm_cols(values):
    count = values.shape[0]
    centred = values - jnp.sum(values, axis=0, keepdims=True) * (1.0 / count)
    var = jnp.sum(centred * centred, axis=0, keepdims=True) * (1.0 / count)
    inv_std = lax.rsqrt(var + epsilon)
    return centred * inv_std, inv_std


def mean_cols(values):
    return jnp.sum(values, axis=0, keepdims=True) * (1.0 / values.shape[0])


def fold(values, width):
    total = values[:, 0:width]
    for at in range(width, values.shape[1], width):
        total = total + values[:, at : at + width]
    return total


def kernel(
    crops,
    groups,
    act,
    cot_arg,
    in_gain_row,
    in_bias_row,
    w,
    wg,
    out_gain_row,
    out_bias_row,
    wo,
    update,
    pair_grad,
    proj_grad,
    gate_grad,
    out_grad,
    in_norm_grad,
    out_norm_grad,
    act_all,
    cot,
    mixed_grad,
    mixed_cols,
    left_part,
    right_part,
    left,
    right,
    tri_r,
    tri_c,
    col_grad,
    normed_sc,
    hat_sc,
    inv_sc,
    sig_a,
    rest_a,
    sig_b,
    rest_b,
    gate_sc,
    slope_sc,
    d_out_sc,
    first_sc,
    d_gate_sc,
    d_normed_sc,
    sums,
    in_sems,
    recv_sem,
    right_sem,
    left_sem,
    col_send,
    col_recv,
    w_t,
    eye,
    columns,
    early,
    late,
    early_bufs,
    late_bufs,
    sum_sems,
    swap_sems,
):
    me = lax.axis_index("dap")
    crop = lax.axis_index("dp")
    rows, length, channels = act.shape
    hidden = wo.shape[0]
    cut = min(CUT, rows)
    cuts = rows // cut
    cells = STEP * length

    act_in = pltpu.make_async_copy(act, act_all.at[me], in_sems.at[0])
    cot_in = pltpu.make_async_copy(cot_arg, cot, in_sems.at[1])
    act_in.start()
    cot_in.start()

    barrier = pltpu.get_barrier_semaphore()
    for d in range(1, groups):
        pl.semaphore_signal(
            barrier,
            inc=1,
            device_id={"dap": lax.rem(me + d, groups)},
            device_id_type=pl.DeviceIdType.MESH,
        )
    for d in range(1, crops):
        pl.semaphore_signal(
            barrier,
            inc=1,
            device_id={"dp": lax.rem(crop + d, crops)},
            device_id_type=pl.DeviceIdType.MESH,
        )
    pl.semaphore_wait(barrier, groups + crops - 2)

    def hop(src, block, c, send_sems, to):
        part = pl.ds(c * cut, cut)
        return pltpu.make_async_remote_copy(
            src_ref=src.at[part],
            dst_ref=act_all.at[block, part],
            send_sem=send_sems.at[block, c],
            recv_sem=recv_sem.at[block, c],
            device_id={"dap": to},
            device_id_type=pl.DeviceIdType.MESH,
        )

    def col_copy(d, q):
        peer = lax.rem(me + d, groups)
        at = pl.multiple_of(peer * rows + q * cut, cut)
        mine = pl.multiple_of(me * rows, rows)
        return pltpu.make_async_remote_copy(
            src_ref=mixed_grad.at[:, pl.ds(at, cut), :],
            dst_ref=mixed_cols.at[pl.ds(mine, rows), pl.ds(q * cut, cut), :],
            send_sem=col_send.at[d - 1, q],
            recv_sem=col_recv.at[d - 1, q],
            device_id={"dap": peer},
            device_id_type=pl.DeviceIdType.MESH,
        )

    @pl.when(me + 1 < groups)
    def _():
        for c in range(cuts):
            hop(act, me, c, right_sem, me + 1).start()

    @pl.when(me >= 1)
    def _():
        for c in range(cuts):
            hop(act, me, c, left_sem, me - 1).start()

    def turned(block):
        return jnp.transpose(block.astype(f32)).astype(bf16)

    for n in range(4):
        w_t[n * hidden : (n + 1) * hidden, :] = turned(w[:, n * hidden : (n + 1) * hidden])
    square = (channels, channels)
    eye[...] = (
        (lax.broadcasted_iota(jnp.int32, square, 0) == lax.broadcasted_iota(jnp.int32, square, 1))
        .astype(f32)
        .astype(bf16)
    )
    for n, row in enumerate((in_gain_row, in_bias_row, out_gain_row, out_bias_row)):
        columns[n] = jnp.transpose(jnp.broadcast_to(row[...], square))[:, 0:1]
    in_gain, in_bias, out_gain, out_bias = (columns.at[n] for n in range(4))
    sums[...] = jnp.zeros_like(sums)
    early[...] = jnp.zeros_like(early)
    late[...] = jnp.zeros_like(late)

    def piece_copy(which, stage, bufs, e):
        peer = lax.rem(crop + e, crops)
        sent, got, _, total = bufs
        src, dst = (sent.at[peer], got.at[crop]) if stage == 0 else (total.at[crop],) * 2
        return pltpu.make_async_remote_copy(
            src_ref=src,
            dst_ref=dst,
            send_sem=sum_sems.at[which, stage, 0, e - 1],
            recv_sem=sum_sems.at[which, stage, 1, e - 1],
            device_id={"dp": peer},
            device_id_type=pl.DeviceIdType.MESH,
        )

    def swap_copy(which, bufs, d):
        part = bufs[2]
        return pltpu.make_async_remote_copy(
            src_ref=part.at[me],
            dst_ref=part.at[me],
            send_sem=swap_sems.at[which, 0, d - 1],
            recv_sem=swap_sems.at[which, 1, d - 1],
            device_id={"dap": lax.rem(me + d, groups)},
            device_id_type=pl.DeviceIdType.MESH,
        )

    piece = channels // crops

    def sum_first(which, acc, bufs):
        for p in range(crops):
            bufs[0][p] = acc[p * piece : (p + 1) * piece, :]
        for e in range(1, crops):
            piece_copy(which, 0, bufs, e).start()

    def sum_second(which, bufs):
        total = bufs[0][crop]
        for e in range(1, crops):
            piece_copy(which, 0, bufs, e).wait_recv()
            total = total + bufs[1][lax.rem(crop + crops - e, crops)]
        bufs[2][me] = total
        for d in range(1, groups):
            swap_copy(which, bufs, d).start()

    def sum_third(which, bufs):
        for d in range(1, groups):
            swap_copy(which, bufs, d).wait_recv()
        total = bufs[2][0]
        for g in range(1, groups):
            total = total + bufs[2][g]
        bufs[3][crop] = total * (1.0 / length)
        for e in range(1, crops):
            piece_copy(which, 1, bufs, e).start()

    def sum_last(which, bufs, outs, stats_out):
        for e in range(1, crops):
            piece_copy(which, 1, bufs, e).wait_recv()
        total = jnp.concatenate([bufs[3][p] for p in range(crops)], axis=0)
        at = 0
        for out in outs:
            out[...] = total[:, at : at + out.shape[1]]
            at += out.shape[1]
        turned_stats = jnp.transpose(total[:, at : at + channels])
        stats_out[0:1, :] = turned_stats[0:1]
        stats_out[1:2, :] = turned_stats[8:9]
        for e in range(1, crops):
            piece_copy(which, 0, bufs, e).wait_send()
            piece_copy(which, 1, bufs, e).wait_send()
        for d in range(1, groups):
            swap_copy(which, bufs, d).wait_send()

    def put_stats(acc, first):
        at = acc.shape[1] - channels
        for n in range(2):
            acc[:, at + 8 * n : at + 8 * n + 8] = jnp.broadcast_to(
                jnp.sum(sums[first + n], axis=1, keepdims=True), (channels, 8)
            )

    def normed_of(x):
        hat, inv = norm_cols(mm_t(eye[...], x))
        return hat, inv, (hat * in_gain[...] + in_bias[...]).astype(bf16)

    def put_part(ref, first, values):
        for r in range(STEP):
            ref[pl.ds(first + r, hidden, stride=cut), :] = values[:, r * length : (r + 1) * length]

    def settle(base):
        def body(h, carry):
            frm = pl.ds(pl.multiple_of(h * cut, cut), cut)
            to = pl.ds(pl.multiple_of(h * length + base, cut), cut)
            left[to, :] = left_part[frm, :].astype(bf16)
            right[to, :] = right_part[frm, :].astype(bf16)
            return carry

        lax.fori_loop(0, hidden, body, 0, unroll=8)

    def sides(block, c):
        def body(t, carry):
            x = act_all[block, pl.ds(c * cut + t * STEP, STEP)].reshape(cells, channels)
            _, _, normed = normed_of(x)
            pj = mm(w_t[...], normed)
            put_part(left_part, t * STEP, sigmoid(pj[0:hidden]) * pj[hidden : 2 * hidden])
            put_part(
                right_part, t * STEP, sigmoid(pj[2 * hidden : 3 * hidden]) * pj[3 * hidden : 4 * hidden]
            )
            return carry

        lax.fori_loop(0, cut // STEP, body, 0)
        settle(block * rows + c * cut)

    def own_sides(c):
        def body(t, carry):
            at = c * (cut // STEP) + t
            x = act_all[me, pl.ds(at * STEP, STEP)].reshape(cells, channels)
            hat, inv, normed = normed_of(x)
            hat_sc[at] = hat
            inv_sc[at] = inv
            normed_sc[at] = normed
            pj = mm(w_t[...], normed)
            sa, va = sigmoid(pj[0:hidden]), pj[hidden : 2 * hidden]
            sig_a[at] = sa
            rest_a[at] = va * (1.0 - sa)
            put_part(left_part, t * STEP, sa * va)
            sb, vb = sigmoid(pj[2 * hidden : 3 * hidden]), pj[3 * hidden : 4 * hidden]
            sig_b[at] = sb
            rest_b[at] = vb * (1.0 - sb)
            put_part(right_part, t * STEP, sb * vb)
            return carry

        lax.fori_loop(0, cut // STEP, body, 0)
        settle(me * rows + c * cut)

    def own_gate(t, carry):
        normed = normed_sc[t]
        flat = jnp.concatenate(
            [
                mm_t(eye[...], normed[:, r * length : (r + 1) * length]).astype(bf16)
                for r in range(STEP)
            ],
            axis=0,
        )
        gate = sigmoid(mm(flat, wg[...]))
        grad = cot[pl.ds(t * STEP, STEP)].reshape(cells, channels).astype(f32) * gate
        gate_sc[t] = gate
        slope_sc[t] = grad * (1.0 - gate)
        d_mixed = grad.astype(bf16)
        mixed_grad[pl.ds(t * STEP, STEP)] = d_mixed.reshape(STEP, length, channels)
        d_out = mm_t(wo[...], d_mixed)
        d_out_sc[t] = d_out
        first_sc[t] = mean_cols(d_out * out_gain[...])
        sums[3] += fold(d_out, length)
        return carry

    act_in.wait()
    for c in range(cuts):
        own_sides(c)
    cot_in.wait()
    lax.fori_loop(0, rows // STEP, own_gate, 0)

    for s in range(1, groups):
        low, high = me - s, me + s
        for c in range(cuts):

            @pl.when(low >= 0)
            def _():
                hop(act, low, c, right_sem, me).wait_recv()

                @pl.when(me + 1 < groups)
                def _():
                    hop(act_all.at[low], low, c, right_sem, me + 1).start()

            @pl.when(high < groups)
            def _():
                hop(act, high, c, left_sem, me).wait_recv()

                @pl.when(me >= 1)
                def _():
                    hop(act_all.at[high], high, c, left_sem, me - 1).start()

            if s == groups - 1 and c == cuts - 1:
                for q in range(cuts):
                    for d in range(1, groups):
                        col_copy(d, q).start()

            @pl.when(low >= 0)
            def _():
                sides(low, c)

            @pl.when(high < groups)
            def _():
                sides(high, c)

    mine = pl.multiple_of(me * rows, rows)

    def products(h, carry):
        at = pl.multiple_of(h * length, length)
        l_all = left[pl.ds(at, length), :]
        r_all = right[pl.ds(at, length), :]
        l_own = left[pl.ds(pl.multiple_of(at + mine, rows), rows), :]
        r_own = right[pl.ds(pl.multiple_of(at + mine, rows), rows), :]
        to = pl.ds(pl.multiple_of(h * rows, rows), rows)
        tri_r[to, :] = mm_t(l_own, r_all)
        tri_c[to, :] = mm_t(r_own, l_all)
        return carry

    lax.fori_loop(0, hidden, products, 0, unroll=8)

    def slabs(ref, first):
        return jnp.concatenate(
            [ref[pl.ds(first + r, hidden, stride=rows), :] for r in range(STEP)], axis=1
        )

    def put_slabs(ref, first, values):
        for r in range(STEP):
            ref[pl.ds(first + r, hidden, stride=rows), :] = values[
                :, r * length : (r + 1) * length
            ]

    def row_pass(t, carry):
        first = t * STEP
        hat, inv = norm_cols(slabs(tri_r, first).astype(bf16).astype(f32))
        tri_norm = (hat * out_gain[...] + out_bias[...]).astype(bf16)
        d_out = d_out_sc[t]
        scaled = d_out * hat
        sums[2] += fold(scaled, length)
        second = mean_cols(scaled * out_gain[...])
        put_slabs(tri_r, first, (d_out * out_gain[...] - first_sc[t] - hat * second) * inv)
        flat = jnp.concatenate(
            [
                mm_t(eye[...], tri_norm[:, r * length : (r + 1) * length]).astype(bf16)
                for r in range(STEP)
            ],
            axis=0,
        )
        mixed = mm(flat, wo[...])
        update[pl.ds(first, STEP)] = (gate_sc[t] * mixed).astype(bf16).reshape(STEP, length, channels)
        d_gate = (slope_sc[t] * mixed).astype(bf16)
        d_gate_sc[t] = d_gate
        d_mixed = mixed_grad[pl.ds(first, STEP)].reshape(cells, channels)
        early[:, 0:channels] += mm(normed_sc[t], d_gate)
        early[:, channels : 2 * channels] += mm(tri_norm, d_mixed)
        return carry

    lax.fori_loop(0, rows // STEP, row_pass, 0)

    def back_rows(h, carry):
        r_all = right[pl.ds(pl.multiple_of(h * length, length), length), :]
        to = pl.ds(pl.multiple_of(h * rows, rows), rows)
        tri_r[to, :] = mm(tri_r[to, :].astype(bf16), r_all)
        return carry

    lax.fori_loop(0, hidden, back_rows, 0, unroll=8)

    half = 2 * hidden

    def half_grad(ref, first, sig, rest):
        d_val = slabs(ref, first).astype(bf16).astype(f32) * sig
        return jnp.concatenate([(d_val * rest).astype(bf16), d_val.astype(bf16)], axis=0)

    def left_pass(t, carry):
        d_proj = half_grad(tri_r, t * STEP, sig_a[t], rest_a[t])
        early[:, 2 * channels : 2 * channels + half] += mm_t(normed_sc[t], d_proj)
        d_normed_sc[t] = mm(w[:, 0:half], d_proj) + mm_t(wg[...], d_gate_sc[t])
        return carry

    lax.fori_loop(0, rows // STEP, left_pass, 0)
    put_stats(early, 2)
    sum_first(0, early, early_bufs)

    hat_c, inv_c = d_out_sc, first_sc

    def col_norm(t, carry):
        hat_c[t], inv_c[t] = norm_cols(slabs(tri_c, t * STEP).astype(bf16).astype(f32))
        return carry

    lax.fori_loop(0, rows // STEP, col_norm, 0)

    def columns_of(ref, first):
        return jnp.concatenate(
            [ref[pl.ds(first + r, length, stride=cut), :] for r in range(STEP)], axis=0
        ).astype(bf16)

    for q in range(cuts):

        def unpack_own(t, carry):
            to = pl.ds(pl.multiple_of((mine + t) * cut, cut), cut)
            part = pl.ds(pl.multiple_of(mine + q * cut, cut), cut)
            col_grad[to, :] = mixed_grad[t, part, :].astype(f32)
            return carry

        def unpack(t, carry):
            to = pl.ds(pl.multiple_of(t * cut, cut), cut)
            col_grad[to, :] = mixed_cols[t, q * cut : q * cut + cut, :].astype(f32)
            return carry

        lax.fori_loop(0, rows, unpack_own, 0, unroll=4)
        for d in range(1, groups):
            col_copy(d, q).wait_recv()
        for d in range(1, groups):
            peer = lax.rem(me + d, groups)

            def unpack_peer(t, carry):
                return unpack(peer * rows + t, carry)

            lax.fori_loop(0, rows, unpack_peer, 0, unroll=4)

        def col_pass(t, carry):
            at = q * (cut // STEP) + t
            hat = hat_c[at]
            d_hat = mm_t(wo[...], columns_of(col_grad, t * STEP)) * out_gain[...]
            back = (d_hat - mean_cols(d_hat) - hat * mean_cols(d_hat * hat)) * inv_c[at]
            put_slabs(tri_c, at * STEP, back)
            return carry

        lax.fori_loop(0, cut // STEP, col_pass, 0)

    sum_second(0, early_bufs)

    def back_cols(h, carry):
        l_all = left[pl.ds(pl.multiple_of(h * length, length), length), :]
        to = pl.ds(pl.multiple_of(h * rows, rows), rows)
        tri_c[to, :] = mm(tri_c[to, :].astype(bf16), l_all)
        return carry

    lax.fori_loop(0, hidden, back_cols, 0, unroll=8)
    sum_third(0, early_bufs)

    def right_pass(t, carry):
        d_proj = half_grad(tri_c, t * STEP, sig_b[t], rest_b[t])
        late[:, 0:half] += mm_t(normed_sc[t], d_proj)
        d_normed = mm(w[:, half : 2 * half], d_proj) + d_normed_sc[t]
        sums[0] += fold(d_normed * hat_sc[t], length)
        sums[1] += fold(d_normed, length)
        d_normed_sc[t] = d_normed
        return carry

    lax.fori_loop(0, rows // STEP, right_pass, 0)
    put_stats(late, 0)
    sum_first(1, late, late_bufs)

    def last_pass(t, carry):
        hat = hat_sc[t]
        d_hat = d_normed_sc[t] * in_gain[...]
        back = (d_hat - mean_cols(d_hat) - hat * mean_cols(d_hat * hat)) * inv_sc[t]
        back = back.astype(bf16)
        for r in range(STEP):
            pair_grad[t * STEP + r] = mm_t(
                eye[...], back[:, r * length : (r + 1) * length]
            ).astype(bf16)
        return carry

    lax.fori_loop(0, rows // STEP, last_pass, 0)

    sum_second(1, late_bufs)
    sum_last(0, early_bufs, (gate_grad, out_grad, proj_grad.at[:, 0:half]), out_norm_grad)
    sum_third(1, late_bufs)

    for s in range(groups):
        low, high = me - s, me + s

        @pl.when((low >= 0) & (me + 1 < groups))
        def _():
            for c in range(cuts):
                hop(act, low, c, right_sem, me + 1).wait_send()

        @pl.when((high < groups) & (me >= 1))
        def _():
            for c in range(cuts):
                hop(act, high, c, left_sem, me - 1).wait_send()

    for q in range(cuts):
        for d in range(1, groups):
            col_copy(d, q).wait_send()

    sum_last(1, late_bufs, (proj_grad.at[:, half : 2 * half],), in_norm_grad)


def shards(
    crops,
    groups,
    pair_act,
    pair_cot,
    in_gain,
    in_bias,
    proj_weight,
    gate_weight,
    out_gain,
    out_bias,
    out_weight,
):
    _, rows, length, channels = pair_act.shape
    hidden = out_weight.shape[0]
    act = pair_act.reshape(rows, length, channels)
    cot = pair_cot.reshape(rows, length, channels)
    vmem = pl.BlockSpec(memory_space=pltpu.VMEM)
    anywhere = pl.BlockSpec(memory_space=pl.ANY)
    dma = pltpu.SemaphoreType.DMA
    piece = channels // crops
    cut = min(CUT, rows)
    steps, cells = rows // STEP, STEP * length

    def sum_bufs(width):
        return tuple(pltpu.VMEM((n, piece, width), f32) for n in (crops, crops, groups, crops))

    def per_step(*shape, dtype=f32):
        return pltpu.VMEM((steps, *shape), dtype)

    early_width, late_width = 3 * channels + 2 * hidden, 2 * hidden + channels
    update, pair_grad, *grads = pl.pallas_call(
        functools.partial(kernel, crops, groups),
        out_shape=(
            jax.ShapeDtypeStruct(act.shape, bf16),
            jax.ShapeDtypeStruct(act.shape, bf16),
            jax.ShapeDtypeStruct(proj_weight.shape, f32),
            jax.ShapeDtypeStruct(gate_weight.shape, f32),
            jax.ShapeDtypeStruct(out_weight.shape, f32),
            jax.ShapeDtypeStruct((2, channels), f32),
            jax.ShapeDtypeStruct((2, hidden), f32),
        ),
        in_specs=[anywhere] * 2 + [vmem] * 7,
        out_specs=(vmem,) * 7,
        scratch_shapes=[
            pltpu.VMEM((groups, rows, length, channels), bf16),
            pltpu.VMEM((rows, length, channels), bf16),
            pltpu.VMEM((rows, length, channels), bf16),
            pltpu.VMEM((length, rows, channels), bf16),
            pltpu.VMEM((hidden * cut, length), f32),
            pltpu.VMEM((hidden * cut, length), f32),
            pltpu.VMEM((hidden * length, length), bf16),
            pltpu.VMEM((hidden * length, length), bf16),
            pltpu.VMEM((hidden * rows, length), f32),
            pltpu.VMEM((hidden * rows, length), f32),
            pltpu.VMEM((length * cut, channels), f32),
            per_step(channels, cells, dtype=bf16),
            per_step(channels, cells),
            per_step(1, cells),
            per_step(hidden, cells),
            per_step(hidden, cells),
            per_step(hidden, cells),
            per_step(hidden, cells),
            per_step(cells, channels),
            per_step(cells, channels),
            per_step(hidden, cells),
            per_step(1, cells),
            per_step(cells, channels, dtype=bf16),
            per_step(channels, cells),
            pltpu.VMEM((4, channels, length), f32),
            dma((2,)),
            dma((groups, rows // cut)),
            dma((groups, rows // cut)),
            dma((groups, rows // cut)),
            dma((groups - 1, rows // cut)),
            dma((groups - 1, rows // cut)),
            pltpu.VMEM((4 * hidden, channels), bf16),
            pltpu.VMEM((channels, channels), bf16),
            pltpu.VMEM((4, channels, 1), f32),
            pltpu.VMEM((channels, early_width), f32),
            pltpu.VMEM((channels, late_width), f32),
            sum_bufs(early_width),
            sum_bufs(late_width),
            dma((2, 2, 2, crops - 1)),
            dma((2, 2, groups - 1)),
        ],
        compiler_params=pltpu.CompilerParams(
            collective_id=0, has_side_effects=True, vmem_limit_bytes=60 * 1024 * 1024
        ),
        name="tri",
    )(
        act,
        cot,
        in_gain.reshape(1, channels),
        in_bias.reshape(1, channels),
        proj_weight,
        gate_weight,
        out_gain.reshape(1, hidden),
        out_bias.reshape(1, hidden),
        out_weight,
    )
    return (update.reshape(pair_act.shape), pair_grad.reshape(pair_act.shape), *grads)


def solution(mesh):
    placed = (P("dp", "dap", None, None),) * 2 + (P(),) * 7
    return jax.shard_map(
        functools.partial(shards, mesh.shape["dp"], mesh.shape["dap"]),
        mesh=mesh,
        in_specs=placed,
        out_specs=(P("dp", "dap", None, None), P("dp", "dap", None, None), P(), P(), P(), P(), P()),
        check_vma=False,
    )
```

```python
import functools

import jax
import jax.numpy as jnp
from jax import lax
from jax.experimental import pallas as pl
from jax.experimental.pallas import tpu as pltpu
from jax.sharding import PartitionSpec as P

epsilon = 1e-05
f32 = jnp.float32
bf16 = jnp.bfloat16
STEP = 8
CUT = 16


def mm(a, b):
    return jnp.dot(a, b, preferred_element_type=f32)


def mm_t(a, b):
    return lax.dot_general(a, b, (((1,), (1,)), ((), ())), preferred_element_type=f32)


def sigmoid(v):
    return 0.5 * jnp.tanh(0.5 * v) + 0.5


def norm_cols(values):
    count = values.shape[0]
    centred = values - jnp.sum(values, axis=0, keepdims=True) * (1.0 / count)
    var = jnp.sum(centred * centred, axis=0, keepdims=True) * (1.0 / count)
    inv_std = lax.rsqrt(var + epsilon)
    return centred * inv_std, inv_std


def mean_cols(values):
    return jnp.sum(values, axis=0, keepdims=True) * (1.0 / values.shape[0])


def fold(values, width):
    total = values[:, 0:width]
    for at in range(width, values.shape[1], width):
        total = total + values[:, at : at + width]
    return total


def kernel(
    crops,
    groups,
    act,
    cot_arg,
    in_gain_row,
    in_bias_row,
    w,
    wg,
    out_gain_row,
    out_bias_row,
    wo,
    update_out,
    pair_grad_out,
    proj_grad_out,
    gate_grad_out,
    out_grad_out,
    in_norm_grad_out,
    out_norm_grad_out,
    act_all,
    cot,
    mixed_grad,
    mixed_cols,
    left_part,
    right_part,
    left,
    right,
    tri_r,
    tri_c,
    col_grad,
    normed_sc,
    hat_sc,
    inv_sc,
    sig_a,
    rest_a,
    sig_b,
    rest_b,
    gate_sc,
    slope_sc,
    d_out_sc,
    first_sc,
    d_mixed_sc,
    update_sc,
    d_gate_sc,
    d_normed_sc,
    sums,
    in_sems,
    recv_sem,
    right_sem,
    left_sem,
    col_send,
    col_recv,
    w_t,
    wg_t,
    wo_t,
    eye,
    columns,
    early,
    late,
    early_bufs,
    late_bufs,
    sum_sems,
    swap_sems,
    update,
    pair_grad,
    proj_grad,
    gate_grad,
    out_grad,
    in_norm_grad,
    out_norm_grad,
    out_sems,
):
    me = lax.axis_index("dap")
    crop = lax.axis_index("dp")
    rows, length, channels = act.shape
    hidden = wo.shape[0]
    cut = min(CUT, rows)
    cuts = rows // cut
    cells = STEP * length

    act_in = pltpu.make_async_copy(act, act_all.at[me], in_sems.at[0])
    cot_in = pltpu.make_async_copy(cot_arg, cot, in_sems.at[1])
    results = (
        (update, update_out),
        (pair_grad, pair_grad_out),
        (proj_grad, proj_grad_out),
        (gate_grad, gate_grad_out),
        (out_grad, out_grad_out),
        (in_norm_grad, in_norm_grad_out),
        (out_norm_grad, out_norm_grad_out),
    )

    def copy_out(n):
        return pltpu.make_async_copy(*results[n], out_sems.at[n])

    act_in.start()
    cot_in.start()

    barrier = pltpu.get_barrier_semaphore()
    for d in range(1, groups):
        pl.semaphore_signal(
            barrier,
            inc=1,
            device_id={"dap": lax.rem(me + d, groups)},
            device_id_type=pl.DeviceIdType.MESH,
        )
    for d in range(1, crops):
        pl.semaphore_signal(
            barrier,
            inc=1,
            device_id={"dp": lax.rem(crop + d, crops)},
            device_id_type=pl.DeviceIdType.MESH,
        )
    pl.semaphore_wait(barrier, groups + crops - 2)

    def hop(src, block, c, send_sems, to):
        part = pl.ds(c * cut, cut)
        return pltpu.make_async_remote_copy(
            src_ref=src.at[part],
            dst_ref=act_all.at[block, part],
            send_sem=send_sems.at[block, c],
            recv_sem=recv_sem.at[block, c],
            device_id={"dap": to},
            device_id_type=pl.DeviceIdType.MESH,
        )

    def col_copy(d, q):
        peer = lax.rem(me + d, groups)
        at = pl.multiple_of(peer * rows + q * cut, cut)
        mine = pl.multiple_of(me * rows, rows)
        return pltpu.make_async_remote_copy(
            src_ref=mixed_grad.at[:, pl.ds(at, cut), :],
            dst_ref=mixed_cols.at[pl.ds(mine, rows), pl.ds(q * cut, cut), :],
            send_sem=col_send.at[d - 1, q],
            recv_sem=col_recv.at[d - 1, q],
            device_id={"dap": peer},
            device_id_type=pl.DeviceIdType.MESH,
        )

    @pl.when(me + 1 < groups)
    def _():
        for c in range(cuts):
            hop(act, me, c, right_sem, me + 1).start()

    @pl.when(me >= 1)
    def _():
        for c in range(cuts):
            hop(act, me, c, left_sem, me - 1).start()

    def turned(block):
        return jnp.transpose(block.astype(f32)).astype(bf16)

    for n in range(4):
        w_t[n * hidden : (n + 1) * hidden, :] = turned(w[:, n * hidden : (n + 1) * hidden])
    wg_t[...] = turned(wg[...])
    wo_t[...] = turned(wo[...])
    square = (channels, channels)
    eye[...] = (
        (lax.broadcasted_iota(jnp.int32, square, 0) == lax.broadcasted_iota(jnp.int32, square, 1))
        .astype(f32)
        .astype(bf16)
    )
    for n, row in enumerate((in_gain_row, in_bias_row, out_gain_row, out_bias_row)):
        columns[n] = jnp.transpose(jnp.broadcast_to(row[...], square))[:, 0:1]
    in_gain, in_bias, out_gain, out_bias = (columns.at[n] for n in range(4))
    sums[...] = jnp.zeros_like(sums)
    early[...] = jnp.zeros_like(early)
    late[...] = jnp.zeros_like(late)

    def piece_copy(which, stage, bufs, e):
        peer = lax.rem(crop + e, crops)
        sent, got, _, total = bufs
        src, dst = (sent.at[peer], got.at[crop]) if stage == 0 else (total.at[crop],) * 2
        return pltpu.make_async_remote_copy(
            src_ref=src,
            dst_ref=dst,
            send_sem=sum_sems.at[which, stage, 0, e - 1],
            recv_sem=sum_sems.at[which, stage, 1, e - 1],
            device_id={"dp": peer},
            device_id_type=pl.DeviceIdType.MESH,
        )

    def swap_copy(which, bufs, d):
        part = bufs[2]
        return pltpu.make_async_remote_copy(
            src_ref=part.at[me],
            dst_ref=part.at[me],
            send_sem=swap_sems.at[which, 0, d - 1],
            recv_sem=swap_sems.at[which, 1, d - 1],
            device_id={"dap": lax.rem(me + d, groups)},
            device_id_type=pl.DeviceIdType.MESH,
        )

    piece = channels // crops

    def sum_first(which, acc, bufs):
        for p in range(crops):
            bufs[0][p] = acc[p * piece : (p + 1) * piece, :].astype(bf16)
        for e in range(1, crops):
            piece_copy(which, 0, bufs, e).start()

    def sum_second(which, bufs):
        total = bufs[0][crop].astype(f32)
        for e in range(1, crops):
            piece_copy(which, 0, bufs, e).wait_recv()
            total = total + bufs[1][lax.rem(crop + crops - e, crops)]
        bufs[2][me] = total.astype(bf16)
        for d in range(1, groups):
            swap_copy(which, bufs, d).start()

    def sum_third(which, bufs):
        for d in range(1, groups):
            swap_copy(which, bufs, d).wait_recv()
        total = bufs[2][0].astype(f32)
        for g in range(1, groups):
            total = total + bufs[2][g]
        bufs[3][crop] = (total * (1.0 / length)).astype(bf16)
        for e in range(1, crops):
            piece_copy(which, 1, bufs, e).start()

    def sum_last(which, bufs, outs, stats_out):
        for e in range(1, crops):
            piece_copy(which, 1, bufs, e).wait_recv()
        total = jnp.concatenate([bufs[3][p] for p in range(crops)], axis=0).astype(f32)
        at = 0
        for out in outs:
            out[...] = total[:, at : at + out.shape[1]]
            at += out.shape[1]
        turned_stats = jnp.transpose(total[:, at : at + channels])
        stats_out[0:1, :] = turned_stats[0:1]
        stats_out[1:2, :] = turned_stats[8:9]
        for e in range(1, crops):
            piece_copy(which, 0, bufs, e).wait_send()
            piece_copy(which, 1, bufs, e).wait_send()
        for d in range(1, groups):
            swap_copy(which, bufs, d).wait_send()

    def put_stats(acc, first):
        at = acc.shape[1] - channels
        for n in range(2):
            acc[:, at + 8 * n : at + 8 * n + 8] = jnp.broadcast_to(
                jnp.sum(sums[first + n], axis=1, keepdims=True), (channels, 8)
            )

    def normed_of(x):
        hat, inv = norm_cols(mm_t(eye[...], x))
        return hat, inv, (hat * in_gain[...] + in_bias[...]).astype(bf16)

    def put_part(ref, first, values):
        for r in range(STEP):
            ref[pl.ds(first + r, hidden, stride=cut), :] = values[:, r * length : (r + 1) * length]

    def settle(base):
        def body(h, carry):
            frm = pl.ds(pl.multiple_of(h * cut, cut), cut)
            to = pl.ds(pl.multiple_of(h * length + base, cut), cut)
            left[to, :] = left_part[frm, :].astype(bf16)
            right[to, :] = right_part[frm, :].astype(bf16)
            return carry

        lax.fori_loop(0, hidden, body, 0, unroll=8)

    def sides(block, c):
        def body(t, carry):
            x = act_all[block, pl.ds(c * cut + t * STEP, STEP)].reshape(cells, channels)
            _, _, normed = normed_of(x)
            pj = mm(w_t[...], normed)
            put_part(left_part, t * STEP, sigmoid(pj[0:hidden]) * pj[hidden : 2 * hidden])
            put_part(
                right_part, t * STEP, sigmoid(pj[2 * hidden : 3 * hidden]) * pj[3 * hidden : 4 * hidden]
            )
            return carry

        lax.fori_loop(0, cut // STEP, body, 0)
        settle(block * rows + c * cut)

    def own_sides(c):
        def body(t, carry):
            at = c * (cut // STEP) + t
            x = act_all[me, pl.ds(at * STEP, STEP)].reshape(cells, channels)
            hat, inv, normed = normed_of(x)
            hat_sc[at] = hat
            inv_sc[at] = inv
            normed_sc[at] = normed
            pj = mm(w_t[...], normed)
            sa, va = sigmoid(pj[0:hidden]), pj[hidden : 2 * hidden]
            sig_a[at] = sa
            rest_a[at] = va * (1.0 - sa)
            put_part(left_part, t * STEP, sa * va)
            sb, vb = sigmoid(pj[2 * hidden : 3 * hidden]), pj[3 * hidden : 4 * hidden]
            sig_b[at] = sb
            rest_b[at] = vb * (1.0 - sb)
            put_part(right_part, t * STEP, sb * vb)
            return carry

        lax.fori_loop(0, cut // STEP, body, 0)
        settle(me * rows + c * cut)

    def own_gate(t, carry):
        gate = sigmoid(mm(wg_t[...], normed_sc[t]))
        cot_t = mm_t(eye[...], cot[pl.ds(t * STEP, STEP)].reshape(cells, channels))
        grad = cot_t * gate
        gate_sc[t] = gate
        slope_sc[t] = grad * (1.0 - gate)
        d_mixed = grad.astype(bf16)
        d_mixed_sc[t] = d_mixed
        for r in range(STEP):
            mixed_grad[t * STEP + r] = mm_t(
                eye[...], d_mixed[:, r * length : (r + 1) * length]
            ).astype(bf16)
        d_out = mm(wo[...], d_mixed)
        d_out_sc[t] = d_out
        first_sc[t] = mean_cols(d_out * out_gain[...])
        sums[3] += fold(d_out, length)
        return carry

    act_in.wait()
    for c in range(cuts):
        own_sides(c)
    cot_in.wait()
    lax.fori_loop(0, rows // STEP, own_gate, 0)

    for s in range(1, groups):
        low, high = me - s, me + s
        for c in range(cuts):

            @pl.when(low >= 0)
            def _():
                hop(act, low, c, right_sem, me).wait_recv()

                @pl.when(me + 1 < groups)
                def _():
                    hop(act_all.at[low], low, c, right_sem, me + 1).start()

            @pl.when(high < groups)
            def _():
                hop(act, high, c, left_sem, me).wait_recv()

                @pl.when(me >= 1)
                def _():
                    hop(act_all.at[high], high, c, left_sem, me - 1).start()

            if s == groups - 1 and c == cuts - 1:
                for q in range(cuts):
                    for d in range(1, groups):
                        col_copy(d, q).start()

            @pl.when(low >= 0)
            def _():
                sides(low, c)

            @pl.when(high < groups)
            def _():
                sides(high, c)

    mine = pl.multiple_of(me * rows, rows)

    def products(h, carry):
        at = pl.multiple_of(h * length, length)
        l_all = left[pl.ds(at, length), :]
        r_all = right[pl.ds(at, length), :]
        l_own = left[pl.ds(pl.multiple_of(at + mine, rows), rows), :]
        r_own = right[pl.ds(pl.multiple_of(at + mine, rows), rows), :]
        to = pl.ds(pl.multiple_of(h * rows, rows), rows)
        both = mm_t(
            jnp.concatenate([l_own, r_own], axis=0), jnp.concatenate([r_all, l_all], axis=0)
        )
        tri_r[to, :] = both[0:rows, 0:length]
        tri_c[to, :] = both[rows : 2 * rows, length : 2 * length]
        return carry

    lax.fori_loop(0, hidden, products, 0, unroll=16)

    def slabs(ref, first):
        return jnp.concatenate(
            [ref[pl.ds(first + r, hidden, stride=rows), :] for r in range(STEP)], axis=1
        )

    def put_slabs(ref, first, values):
        for r in range(STEP):
            ref[pl.ds(first + r, hidden, stride=rows), :] = values[
                :, r * length : (r + 1) * length
            ]

    def row_pass(t, carry):
        first = t * STEP
        hat, inv = norm_cols(slabs(tri_r, first).astype(bf16).astype(f32))
        tri_norm = (hat * out_gain[...] + out_bias[...]).astype(bf16)
        d_out = d_out_sc[t]
        scaled = d_out * hat
        sums[2] += fold(scaled, length)
        second = mean_cols(scaled * out_gain[...])
        put_slabs(tri_r, first, (d_out * out_gain[...] - first_sc[t] - hat * second) * inv)
        mixed = mm(wo_t[...], tri_norm)
        update_sc[t] = (gate_sc[t] * mixed).astype(bf16)
        d_gate = (slope_sc[t] * mixed).astype(bf16)
        d_gate_sc[t] = d_gate
        early[:, 0:channels] += mm_t(normed_sc[t], d_gate)
        early[:, channels : 2 * channels] += mm_t(tri_norm, d_mixed_sc[t])
        return carry

    lax.fori_loop(0, rows // STEP, row_pass, 0)

    def back_rows(h, carry):
        r_all = right[pl.ds(pl.multiple_of(h * length, length), length), :]
        to = pl.ds(pl.multiple_of(h * rows, rows), rows)
        tri_r[to, :] = mm(tri_r[to, :].astype(bf16), r_all)
        return carry

    lax.fori_loop(0, hidden, back_rows, 0, unroll=8)

    half = 2 * hidden

    def half_grad(ref, first, sig, rest):
        d_val = slabs(ref, first).astype(bf16).astype(f32) * sig
        return jnp.concatenate([(d_val * rest).astype(bf16), d_val.astype(bf16)], axis=0)

    def left_pass(t, carry):
        d_proj = half_grad(tri_r, t * STEP, sig_a[t], rest_a[t])
        early[:, 2 * channels : 2 * channels + half] += mm_t(normed_sc[t], d_proj)
        d_normed_sc[t] = mm(w[:, 0:half], d_proj) + mm(wg[...], d_gate_sc[t])
        return carry

    lax.fori_loop(0, rows // STEP, left_pass, 0)
    put_stats(early, 2)
    sum_first(0, early, early_bufs)

    hat_c, inv_c = d_out_sc, first_sc

    def col_norm(t, carry):
        hat_c[t], inv_c[t] = norm_cols(slabs(tri_c, t * STEP).astype(bf16).astype(f32))
        return carry

    lax.fori_loop(0, rows // STEP, col_norm, 0)

    def columns_of(ref, first):
        return jnp.concatenate(
            [ref[pl.ds(first + r, length, stride=cut), :] for r in range(STEP)], axis=0
        ).astype(bf16)

    for q in range(cuts):

        def unpack_own(t, carry):
            to = pl.ds(pl.multiple_of((mine + t) * cut, cut), cut)
            part = pl.ds(pl.multiple_of(mine + q * cut, cut), cut)
            col_grad[to, :] = mixed_grad[t, part, :].astype(f32)
            return carry

        def unpack(t, carry):
            to = pl.ds(pl.multiple_of(t * cut, cut), cut)
            col_grad[to, :] = mixed_cols[t, q * cut : q * cut + cut, :].astype(f32)
            return carry

        lax.fori_loop(0, rows, unpack_own, 0, unroll=4)
        for d in range(1, groups):
            col_copy(d, q).wait_recv()
        for d in range(1, groups):
            peer = lax.rem(me + d, groups)

            def unpack_peer(t, carry):
                return unpack(peer * rows + t, carry)

            lax.fori_loop(0, rows, unpack_peer, 0, unroll=4)

        def col_pass(t, carry):
            at = q * (cut // STEP) + t
            hat = hat_c[at]
            d_hat = mm_t(wo[...], columns_of(col_grad, t * STEP)) * out_gain[...]
            back = (d_hat - mean_cols(d_hat) - hat * mean_cols(d_hat * hat)) * inv_c[at]
            put_slabs(tri_c, at * STEP, back)
            return carry

        lax.fori_loop(0, cut // STEP, col_pass, 0)

    sum_second(0, early_bufs)

    def back_cols(h, carry):
        l_all = left[pl.ds(pl.multiple_of(h * length, length), length), :]
        to = pl.ds(pl.multiple_of(h * rows, rows), rows)
        tri_c[to, :] = mm(tri_c[to, :].astype(bf16), l_all)
        return carry

    lax.fori_loop(0, hidden, back_cols, 0, unroll=8)
    sum_third(0, early_bufs)

    def right_pass(t, carry):
        d_proj = half_grad(tri_c, t * STEP, sig_b[t], rest_b[t])
        late[:, 0:half] += mm_t(normed_sc[t], d_proj)
        d_normed = mm(w[:, half : 2 * half], d_proj) + d_normed_sc[t]
        sums[0] += fold(d_normed * hat_sc[t], length)
        sums[1] += fold(d_normed, length)
        d_normed_sc[t] = d_normed
        return carry

    lax.fori_loop(0, rows // STEP, right_pass, 0)
    put_stats(late, 0)
    sum_first(1, late, late_bufs)

    def turn_back(values, out, t):
        for r in range(STEP):
            out[t * STEP + r] = mm_t(eye[...], values[:, r * length : (r + 1) * length]).astype(bf16)

    def last_pass(t, carry):
        hat = hat_sc[t]
        d_hat = d_normed_sc[t] * in_gain[...]
        back = (d_hat - mean_cols(d_hat) - hat * mean_cols(d_hat * hat)) * inv_sc[t]
        turn_back(back.astype(bf16), pair_grad, t)
        return carry

    def update_pass(t, carry):
        turn_back(update_sc[t], update, t)
        return carry

    lax.fori_loop(0, rows // STEP, last_pass, 0)
    copy_out(1).start()
    sum_second(1, late_bufs)
    lax.fori_loop(0, rows // STEP, update_pass, 0)
    copy_out(0).start()
    sum_last(0, early_bufs, (gate_grad, out_grad, proj_grad.at[:, 0:half]), out_norm_grad)
    for n in (3, 4, 6):
        copy_out(n).start()
    sum_third(1, late_bufs)

    for s in range(groups):
        low, high = me - s, me + s

        @pl.when((low >= 0) & (me + 1 < groups))
        def _():
            for c in range(cuts):
                hop(act, low, c, right_sem, me + 1).wait_send()

        @pl.when((high < groups) & (me >= 1))
        def _():
            for c in range(cuts):
                hop(act, high, c, left_sem, me - 1).wait_send()

    for q in range(cuts):
        for d in range(1, groups):
            col_copy(d, q).wait_send()

    sum_last(1, late_bufs, (proj_grad.at[:, half : 2 * half],), in_norm_grad)
    for n in (2, 5):
        copy_out(n).start()
    for n in range(7):
        copy_out(n).wait()


def finish(count, *refs):
    ins, outs, held, sems = refs[:count], refs[count : 2 * count], refs[2 * count : -1], refs[-1]
    fetch, store = [], []
    for n in range(count):
        fetch.append(pltpu.make_async_copy(ins[n], held[n], sems.at[0, n]))
        store.append(pltpu.make_async_copy(held[n], outs[n], sems.at[1, n]))
    for copy in fetch:
        copy.start()
    for arrived, copy in zip(fetch, store):
        arrived.wait()
        copy.start()
    for copy in store:
        copy.wait()


def shards(
    crops,
    groups,
    pair_act,
    pair_cot,
    in_gain,
    in_bias,
    proj_weight,
    gate_weight,
    out_gain,
    out_bias,
    out_weight,
):
    _, rows, length, channels = pair_act.shape
    hidden = out_weight.shape[0]
    act = pair_act.reshape(rows, length, channels)
    cot = pair_cot.reshape(rows, length, channels)
    vmem = pl.BlockSpec(memory_space=pltpu.VMEM)
    anywhere = pl.BlockSpec(memory_space=pl.ANY)
    dma = pltpu.SemaphoreType.DMA
    piece = channels // crops
    cut = min(CUT, rows)
    steps, cells = rows // STEP, STEP * length

    def sum_bufs(width):
        return tuple(pltpu.VMEM((n, piece, width), bf16) for n in (crops, crops, groups, crops))

    def per_step(*shape, dtype=f32):
        return pltpu.VMEM((steps, *shape), dtype)

    early_width, late_width = 3 * channels + 2 * hidden, 2 * hidden + channels
    shapes = (
        jax.ShapeDtypeStruct(act.shape, bf16),
        jax.ShapeDtypeStruct(act.shape, bf16),
        jax.ShapeDtypeStruct(proj_weight.shape, f32),
        jax.ShapeDtypeStruct(gate_weight.shape, f32),
        jax.ShapeDtypeStruct(out_weight.shape, f32),
        jax.ShapeDtypeStruct((2, channels), f32),
        jax.ShapeDtypeStruct((2, hidden), f32),
    )
    results = pl.pallas_call(
        functools.partial(kernel, crops, groups),
        out_shape=shapes,
        in_specs=[anywhere] * 2 + [vmem] * 7,
        out_specs=(anywhere,) * 7,
        scratch_shapes=[
            pltpu.VMEM((groups, rows, length, channels), bf16),
            pltpu.VMEM((rows, length, channels), bf16),
            pltpu.VMEM((rows, length, channels), bf16),
            pltpu.VMEM((length, rows, channels), bf16),
            pltpu.VMEM((hidden * cut, length), f32),
            pltpu.VMEM((hidden * cut, length), f32),
            pltpu.VMEM((hidden * length, length), bf16),
            pltpu.VMEM((hidden * length, length), bf16),
            pltpu.VMEM((hidden * rows, length), f32),
            pltpu.VMEM((hidden * rows, length), f32),
            pltpu.VMEM((length * cut, channels), f32),
            per_step(channels, cells, dtype=bf16),
            per_step(channels, cells),
            per_step(1, cells),
            per_step(hidden, cells),
            per_step(hidden, cells),
            per_step(hidden, cells),
            per_step(hidden, cells),
            per_step(channels, cells),
            per_step(channels, cells),
            per_step(hidden, cells),
            per_step(1, cells),
            per_step(channels, cells, dtype=bf16),
            per_step(channels, cells, dtype=bf16),
            per_step(channels, cells, dtype=bf16),
            per_step(channels, cells),
            pltpu.VMEM((4, channels, length), f32),
            dma((2,)),
            dma((groups, rows // cut)),
            dma((groups, rows // cut)),
            dma((groups, rows // cut)),
            dma((groups - 1, rows // cut)),
            dma((groups - 1, rows // cut)),
            pltpu.VMEM((4 * hidden, channels), bf16),
            pltpu.VMEM((channels, channels), bf16),
            pltpu.VMEM((channels, hidden), bf16),
            pltpu.VMEM((channels, channels), bf16),
            pltpu.VMEM((4, channels, 1), f32),
            pltpu.VMEM((channels, early_width), f32),
            pltpu.VMEM((channels, late_width), f32),
            sum_bufs(early_width),
            sum_bufs(late_width),
            dma((2, 2, 2, crops - 1)),
            dma((2, 2, groups - 1)),
            *(pltpu.VMEM(shape.shape, shape.dtype) for shape in shapes),
            dma((7,)),
        ],
        compiler_params=pltpu.CompilerParams(
            collective_id=0, has_side_effects=True, vmem_limit_bytes=60 * 1024 * 1024
        ),
        name="tri",
    )(
        act,
        cot,
        in_gain.reshape(1, channels),
        in_bias.reshape(1, channels),
        proj_weight,
        gate_weight,
        out_gain.reshape(1, hidden),
        out_bias.reshape(1, hidden),
        out_weight,
    )
    update, pair_grad, *grads = pl.pallas_call(
        functools.partial(finish, 7),
        out_shape=shapes,
        in_specs=[anywhere] * 7,
        out_specs=(anywhere,) * 7,
        scratch_shapes=[*(pltpu.VMEM(shape.shape, shape.dtype) for shape in shapes), dma((2, 7))],
        name="finish",
    )(*results)
    return (update.reshape(pair_act.shape), pair_grad.reshape(pair_act.shape), *grads)


def solution(mesh):
    placed = (P("dp", "dap", None, None),) * 2 + (P(),) * 7
    return jax.shard_map(
        functools.partial(shards, mesh.shape["dp"], mesh.shape["dap"]),
        mesh=mesh,
        in_specs=placed,
        out_specs=(P("dp", "dap", None, None), P("dp", "dap", None, None), P(), P(), P(), P(), P()),
        check_vma=False,
    )
```

```python
import functools

import jax
import jax.numpy as jnp
from jax import lax
from jax.experimental import pallas as pl
from jax.experimental.pallas import tpu as pltpu
from jax.sharding import PartitionSpec as P

epsilon = 1e-05
f32 = jnp.float32
bf16 = jnp.bfloat16
STEP = 8
CUT = 16


def mm(a, b):
    return jnp.dot(a, b, preferred_element_type=f32)


def mm_t(a, b):
    return lax.dot_general(a, b, (((1,), (1,)), ((), ())), preferred_element_type=f32)


def sigmoid(v):
    return 0.5 * jnp.tanh(0.5 * v) + 0.5


def norm_cols(values):
    count = values.shape[0]
    centred = values - jnp.sum(values, axis=0, keepdims=True) * (1.0 / count)
    var = jnp.sum(centred * centred, axis=0, keepdims=True) * (1.0 / count)
    inv_std = lax.rsqrt(var + epsilon)
    return centred * inv_std, inv_std


def mean_cols(values):
    return jnp.sum(values, axis=0, keepdims=True) * (1.0 / values.shape[0])


def fold(values, width):
    total = values[:, 0:width]
    for at in range(width, values.shape[1], width):
        total = total + values[:, at : at + width]
    return total


def kernel(
    crops,
    groups,
    act,
    cot_arg,
    in_gain_arg,
    in_bias_arg,
    w_arg,
    wg_arg,
    out_gain_arg,
    out_bias_arg,
    wo_arg,
    update_out,
    pair_grad_out,
    proj_grad_out,
    gate_grad_out,
    out_grad_out,
    in_norm_grad_out,
    out_norm_grad_out,
    act_all,
    cot,
    mixed_grad,
    mixed_cols,
    left_part,
    right_part,
    left_high,
    right_high,
    left,
    right,
    tri_r,
    tri_c,
    col_grad,
    normed_sc,
    hat_sc,
    inv_sc,
    sig_a,
    rest_a,
    sig_b,
    rest_b,
    gate_sc,
    slope_sc,
    d_out_sc,
    first_sc,
    d_mixed_sc,
    update_sc,
    d_gate_sc,
    d_normed_sc,
    sums,
    in_sems,
    recv_sem,
    right_sem,
    left_sem,
    col_send,
    col_recv,
    w_t,
    wg_t,
    wo_t,
    eye,
    columns,
    early,
    late,
    early_bufs,
    late_bufs,
    sum_sems,
    swap_sems,
    update,
    pair_grad,
    proj_grad,
    gate_grad,
    out_grad,
    in_norm_grad,
    out_norm_grad,
    out_sems,
    in_gain_row,
    in_bias_row,
    w,
    wg,
    out_gain_row,
    out_bias_row,
    wo,
):
    me = lax.axis_index("dap")
    crop = lax.axis_index("dp")
    rows, length, channels = act.shape
    hidden = wo.shape[0]
    cut = min(CUT, rows)
    cuts = rows // cut
    cells = STEP * length
    hops = rows // STEP
    wide = length // 2
    near = jnp.minimum(me, groups - 1 - me)

    def block_in(slot):
        if slot == 0:
            return me
        step = (slot + 1) // 2
        paired = me - step if slot % 2 else me + step
        alone = jnp.where(me == near, me + slot - near, me - slot + near)
        return jnp.where(slot <= 2 * near, paired, alone)

    def slot_of(block):
        step = jnp.abs(block - me)
        paired = jnp.where(block < me, 2 * step - 1, 2 * step)
        return jnp.where(step <= near, paired, near + step)

    spans = [pl.ds(pl.multiple_of(block_in(n) * rows, rows), rows) for n in range(groups)]

    def cells_of(ref, first):
        part = pl.ds(first, STEP)
        return jnp.concatenate([ref[part, span, :] for span in spans], axis=1).reshape(
            cells, channels
        )

    per_cut = cut // STEP
    parts = ((left_part, right_part), (left_high, right_high))

    act_in = pltpu.make_async_copy(act, act_all.at[me], in_sems.at[0])
    cot_in = pltpu.make_async_copy(cot_arg, cot, in_sems.at[1])
    results = (
        (update, update_out),
        (pair_grad, pair_grad_out),
        (proj_grad, proj_grad_out),
        (gate_grad, gate_grad_out),
        (out_grad, out_grad_out),
        (in_norm_grad, in_norm_grad_out),
        (out_norm_grad, out_norm_grad_out),
    )

    def copy_out(n):
        return pltpu.make_async_copy(*results[n], out_sems.at[n])

    small_in = [
        pltpu.make_async_copy(src, dst, in_sems.at[2 + n])
        for n, (src, dst) in enumerate(
            (
                (w_arg, w),
                (wg_arg, wg),
                (wo_arg, wo),
                (in_gain_arg, in_gain_row),
                (in_bias_arg, in_bias_row),
                (out_gain_arg, out_gain_row),
                (out_bias_arg, out_bias_row),
            )
        )
    ]
    act_in.start()
    for copy in small_in:
        copy.start()
    cot_in.start()

    barrier = pltpu.get_barrier_semaphore()
    for d in range(1, groups):
        pl.semaphore_signal(
            barrier,
            inc=1,
            device_id={"dap": lax.rem(me + d, groups)},
            device_id_type=pl.DeviceIdType.MESH,
        )
    for d in range(1, crops):
        pl.semaphore_signal(
            barrier,
            inc=1,
            device_id={"dp": lax.rem(crop + d, crops)},
            device_id_type=pl.DeviceIdType.MESH,
        )
    pl.semaphore_wait(barrier, groups + crops - 2)

    def hop(src, block, c, send_sems, to):
        part = pl.ds(c * STEP, STEP)
        return pltpu.make_async_remote_copy(
            src_ref=src.at[part],
            dst_ref=act_all.at[block, part],
            send_sem=send_sems.at[block, c],
            recv_sem=recv_sem.at[block, c],
            device_id={"dap": to},
            device_id_type=pl.DeviceIdType.MESH,
        )

    def col_copy(d, q):
        peer = lax.rem(me + d, groups)
        at = pl.multiple_of(slot_of(peer) * rows + q * cut, cut)
        mine = pl.multiple_of(me * rows, rows)
        return pltpu.make_async_remote_copy(
            src_ref=mixed_grad.at[:, pl.ds(at, cut), :],
            dst_ref=mixed_cols.at[pl.ds(mine, rows), pl.ds(q * cut, cut), :],
            send_sem=col_send.at[d - 1, q],
            recv_sem=col_recv.at[d - 1, q],
            device_id={"dap": peer},
            device_id_type=pl.DeviceIdType.MESH,
        )

    @pl.when(me + 1 < groups)
    def _():
        for c in range(hops):
            hop(act, me, c, right_sem, me + 1).start()

    @pl.when(me >= 1)
    def _():
        for c in range(hops):
            hop(act, me, c, left_sem, me - 1).start()

    for copy in small_in:
        copy.wait()

    def turned(block):
        return jnp.transpose(block.astype(f32)).astype(bf16)

    for n in range(4):
        w_t[n * hidden : (n + 1) * hidden, :] = turned(w[:, n * hidden : (n + 1) * hidden])
    wg_t[...] = turned(wg[...])
    wo_t[...] = turned(wo[...])
    square = (channels, channels)
    eye[...] = (
        (lax.broadcasted_iota(jnp.int32, square, 0) == lax.broadcasted_iota(jnp.int32, square, 1))
        .astype(f32)
        .astype(bf16)
    )
    for n, row in enumerate((in_gain_row, in_bias_row, out_gain_row, out_bias_row)):
        columns[n] = jnp.transpose(jnp.broadcast_to(row[...], square))[:, 0:1]
    in_gain, in_bias, out_gain, out_bias = (columns.at[n] for n in range(4))
    sums[...] = jnp.zeros_like(sums)
    early[...] = jnp.zeros_like(early)
    late[...] = jnp.zeros_like(late)

    def piece_copy(which, stage, bufs, e):
        peer = lax.rem(crop + e, crops)
        sent, got, _, total = bufs
        src, dst = (sent.at[peer], got.at[crop]) if stage == 0 else (total.at[crop],) * 2
        return pltpu.make_async_remote_copy(
            src_ref=src,
            dst_ref=dst,
            send_sem=sum_sems.at[which, stage, 0, e - 1],
            recv_sem=sum_sems.at[which, stage, 1, e - 1],
            device_id={"dp": peer},
            device_id_type=pl.DeviceIdType.MESH,
        )

    def swap_copy(which, bufs, d):
        part = bufs[2]
        return pltpu.make_async_remote_copy(
            src_ref=part.at[me],
            dst_ref=part.at[me],
            send_sem=swap_sems.at[which, 0, d - 1],
            recv_sem=swap_sems.at[which, 1, d - 1],
            device_id={"dap": lax.rem(me + d, groups)},
            device_id_type=pl.DeviceIdType.MESH,
        )

    piece = channels // crops

    def sum_first(which, acc, bufs):
        for p in range(crops):
            bufs[0][p] = acc[p * piece : (p + 1) * piece, :].astype(bf16)
        for e in range(1, crops):
            piece_copy(which, 0, bufs, e).start()

    def sum_second(which, bufs):
        total = bufs[0][crop].astype(f32)
        for e in range(1, crops):
            piece_copy(which, 0, bufs, e).wait_recv()
            total = total + bufs[1][lax.rem(crop + crops - e, crops)]
        bufs[2][me] = total.astype(bf16)
        for d in range(1, groups):
            swap_copy(which, bufs, d).start()

    def sum_third(which, bufs):
        for d in range(1, groups):
            swap_copy(which, bufs, d).wait_recv()
        total = bufs[2][0].astype(f32)
        for g in range(1, groups):
            total = total + bufs[2][g]
        bufs[3][crop] = (total * (1.0 / length)).astype(bf16)
        for e in range(1, crops):
            piece_copy(which, 1, bufs, e).start()

    def sum_last(which, bufs, outs, stats_out):
        for e in range(1, crops):
            piece_copy(which, 1, bufs, e).wait_recv()
        total = jnp.concatenate([bufs[3][p] for p in range(crops)], axis=0).astype(f32)
        at = 0
        for out in outs:
            out[...] = total[:, at : at + out.shape[1]]
            at += out.shape[1]
        turned_stats = jnp.transpose(total[:, at : at + channels])
        stats_out[0:1, :] = turned_stats[0:1]
        stats_out[1:2, :] = turned_stats[8:9]
        for e in range(1, crops):
            piece_copy(which, 0, bufs, e).wait_send()
            piece_copy(which, 1, bufs, e).wait_send()
        for d in range(1, groups):
            swap_copy(which, bufs, d).wait_send()

    def put_stats(acc, first):
        at = acc.shape[1] - channels
        for n in range(2):
            acc[:, at + 8 * n : at + 8 * n + 8] = jnp.broadcast_to(
                jnp.sum(sums[first + n], axis=1, keepdims=True), (channels, 8)
            )

    def normed_of(x):
        hat, inv = norm_cols(mm_t(eye[...], x))
        return hat, inv, (hat * in_gain[...] + in_bias[...]).astype(bf16)

    def put_part(ref, first, values):
        for r in range(STEP):
            ref[pl.ds(first + r, hidden, stride=cut), :] = values[:, r * length : (r + 1) * length]

    def settle(side, base):
        left_part, right_part = parts[side]

        def body(h, carry):
            frm = pl.ds(pl.multiple_of(h * cut, cut), cut)
            to = pl.ds(pl.multiple_of(h * length + base, cut), cut)
            left[to, :] = left_part[frm, :].astype(bf16)
            right[to, :] = right_part[frm, :].astype(bf16)
            return carry

        lax.fori_loop(0, hidden, body, 0, unroll=8)

    def sides(side, block, c):
        left_part, right_part = parts[side]
        x = cells_of(act_all.at[block], c * STEP)
        _, _, normed = normed_of(x)
        pj = mm(w_t[...], normed)
        first = c % per_cut * STEP
        put_part(left_part, first, sigmoid(pj[0:hidden]) * pj[hidden : 2 * hidden])
        put_part(
            right_part, first, sigmoid(pj[2 * hidden : 3 * hidden]) * pj[3 * hidden : 4 * hidden]
        )
        if c % per_cut == per_cut - 1:
            settle(side, slot_of(block) * rows + c // per_cut * cut)

    def own_sides(c):
        left_part, right_part = parts[0]

        def body(t, carry):
            at = c * (cut // STEP) + t
            x = cells_of(act_all.at[me], at * STEP)
            hat, inv, normed = normed_of(x)
            hat_sc[at] = hat
            inv_sc[at] = inv
            normed_sc[at] = normed
            pj = mm(w_t[...], normed)
            sa, va = sigmoid(pj[0:hidden]), pj[hidden : 2 * hidden]
            sig_a[at] = sa
            rest_a[at] = va * (1.0 - sa)
            put_part(left_part, t * STEP, sa * va)
            sb, vb = sigmoid(pj[2 * hidden : 3 * hidden]), pj[3 * hidden : 4 * hidden]
            sig_b[at] = sb
            rest_b[at] = vb * (1.0 - sb)
            put_part(right_part, t * STEP, sb * vb)
            return carry

        lax.fori_loop(0, cut // STEP, body, 0)
        settle(0, c * cut)

    def own_gate(t, carry):
        gate = sigmoid(mm(wg_t[...], normed_sc[t]))
        cot_t = mm_t(eye[...], cells_of(cot, t * STEP))
        grad = cot_t * gate
        gate_sc[t] = gate
        slope_sc[t] = grad * (1.0 - gate)
        d_mixed = grad.astype(bf16)
        d_mixed_sc[t] = d_mixed
        for r in range(STEP):
            mixed_grad[t * STEP + r] = mm_t(
                eye[...], d_mixed[:, r * length : (r + 1) * length]
            ).astype(bf16)
        d_out = mm(wo[...], d_mixed)
        d_out_sc[t] = d_out
        first_sc[t] = mean_cols(d_out * out_gain[...])
        sums[3] += fold(d_out, length)
        return carry

    def at_end(device):
        return (device == 0) | (device == groups - 1)

    def send_cols(from_end, to_end):
        for q in range(cuts):
            for d in range(1, groups):
                peer_at_end = at_end(lax.rem(me + d, groups))

                @pl.when((at_end(me) == from_end) & (peer_at_end == to_end))
                def _():
                    col_copy(d, q).start()

    act_in.wait()
    for c in range(cuts):
        own_sides(c)
    cot_in.wait()
    lax.fori_loop(0, rows // STEP, own_gate, 0)

    def products(late_half):
        def body(h, carry):
            at = h * length
            half_rows = pl.ds(pl.multiple_of(at + late_half * wide, wide), wide)
            own = pl.ds(pl.multiple_of(at, rows), rows)
            to = pl.ds(pl.multiple_of(h * rows, rows), rows)
            sides_of = [right[half_rows, :], left[half_rows, :]]
            both = mm_t(
                jnp.concatenate([left[own, :], right[own, :]], axis=0),
                jnp.concatenate(sides_of[::-1] if late_half else sides_of, axis=0),
            )
            row_lanes = slice(wide, length) if late_half else slice(0, wide)
            col_lanes = slice(0, wide) if late_half else slice(wide, length)
            tri_r[to, row_lanes] = both[0:rows, row_lanes]
            tri_c[to, col_lanes] = both[rows : 2 * rows, col_lanes]
            return carry

        lax.fori_loop(0, hidden, body, 0, unroll=16)

    for s in range(1, groups):
        low, high = me - s, me + s
        for c in range(hops):

            @pl.when(low >= 0)
            def _():
                hop(act, low, c, right_sem, me).wait_recv()

                @pl.when(me + 1 < groups)
                def _():
                    hop(act_all.at[low], low, c, right_sem, me + 1).start()

            @pl.when(high < groups)
            def _():
                hop(act, high, c, left_sem, me).wait_recv()

                @pl.when(me >= 1)
                def _():
                    hop(act_all.at[high], high, c, left_sem, me - 1).start()

            if s == groups - 1 and c == hops - 1:
                send_cols(True, True)
                send_cols(True, False)
                send_cols(False, False)
                send_cols(False, True)

            @pl.when(low >= 0)
            def _():
                sides(0, low, c)

            @pl.when(high < groups)
            def _():
                sides(1, high, c)

        if s == max(1, groups // 2):
            products(0)

    products(1)

    def slabs(ref, first):
        return jnp.concatenate(
            [ref[pl.ds(first + r, hidden, stride=rows), :] for r in range(STEP)], axis=1
        )

    def put_slabs(ref, first, values):
        for r in range(STEP):
            ref[pl.ds(first + r, hidden, stride=rows), :] = values[
                :, r * length : (r + 1) * length
            ]

    def row_pass(t, carry):
        first = t * STEP
        hat, inv = norm_cols(slabs(tri_r, first).astype(bf16).astype(f32))
        tri_norm = (hat * out_gain[...] + out_bias[...]).astype(bf16)
        d_out = d_out_sc[t]
        scaled = d_out * hat
        sums[2] += fold(scaled, length)
        second = mean_cols(scaled * out_gain[...])
        put_slabs(tri_r, first, (d_out * out_gain[...] - first_sc[t] - hat * second) * inv)
        mixed = mm(wo_t[...], tri_norm)
        update_sc[t] = (gate_sc[t] * mixed).astype(bf16)
        d_gate = (slope_sc[t] * mixed).astype(bf16)
        d_gate_sc[t] = d_gate
        early[:, 0:channels] += mm_t(normed_sc[t], d_gate)
        early[:, channels : 2 * channels] += mm_t(tri_norm, d_mixed_sc[t])
        return carry

    lax.fori_loop(0, rows // STEP, row_pass, 0)

    def back_rows(h, carry):
        r_all = right[pl.ds(pl.multiple_of(h * length, length), length), :]
        to = pl.ds(pl.multiple_of(h * rows, rows), rows)
        tri_r[to, :] = mm(tri_r[to, :].astype(bf16), r_all)
        return carry

    lax.fori_loop(0, hidden, back_rows, 0, unroll=8)

    half = 2 * hidden

    def half_grad(ref, first, sig, rest):
        d_val = slabs(ref, first).astype(bf16).astype(f32) * sig
        return jnp.concatenate([(d_val * rest).astype(bf16), d_val.astype(bf16)], axis=0)

    def left_pass(t, carry):
        d_proj = half_grad(tri_r, t * STEP, sig_a[t], rest_a[t])
        early[:, 2 * channels : 2 * channels + half] += mm_t(normed_sc[t], d_proj)
        d_normed_sc[t] = mm(w[:, 0:half], d_proj) + mm(wg[...], d_gate_sc[t])
        return carry

    lax.fori_loop(0, rows // STEP, left_pass, 0)
    put_stats(early, 2)
    sum_first(0, early, early_bufs)

    hat_c, inv_c = d_out_sc, first_sc

    def col_norm(t, carry):
        hat_c[t], inv_c[t] = norm_cols(slabs(tri_c, t * STEP).astype(bf16).astype(f32))
        return carry

    lax.fori_loop(0, rows // STEP, col_norm, 0)

    def columns_of(ref, first):
        return jnp.concatenate(
            [ref[pl.ds(first + r, length, stride=cut), :] for r in range(STEP)], axis=0
        ).astype(bf16)

    for q in range(cuts):

        def unpack_own(t, carry):
            to = pl.ds(pl.multiple_of((wide + t) * cut, cut), cut)
            col_grad[to, :] = mixed_grad[t, q * cut : q * cut + cut, :].astype(f32)
            return carry

        lax.fori_loop(0, rows, unpack_own, 0, unroll=4)
        for d in range(1, groups):
            col_copy(d, q).wait_recv()
        for d in range(1, groups):
            peer = lax.rem(me + d, groups)

            at = lax.rem(slot_of(peer) * rows + wide, length)

            def unpack_peer(t, carry):
                to = pl.ds(pl.multiple_of((at + t) * cut, cut), cut)
                col_grad[to, :] = mixed_cols[peer * rows + t, q * cut : q * cut + cut, :].astype(f32)
                return carry

            lax.fori_loop(0, rows, unpack_peer, 0, unroll=4)

        def col_pass(t, carry):
            at = q * (cut // STEP) + t
            hat = hat_c[at]
            d_hat = mm_t(wo[...], columns_of(col_grad, t * STEP)) * out_gain[...]
            back = (d_hat - mean_cols(d_hat) - hat * mean_cols(d_hat * hat)) * inv_c[at]
            put_slabs(tri_c, at * STEP, back)
            return carry

        lax.fori_loop(0, cut // STEP, col_pass, 0)

    sum_second(0, early_bufs)

    def back_cols(h, carry):
        at = h * length
        l_all = jnp.concatenate(
            [left[pl.ds(pl.multiple_of(at + n * wide, wide), wide), :] for n in (1, 0)], axis=0
        )
        to = pl.ds(pl.multiple_of(h * rows, rows), rows)
        tri_c[to, :] = mm(tri_c[to, :].astype(bf16), l_all)
        return carry

    lax.fori_loop(0, hidden, back_cols, 0, unroll=8)
    sum_third(0, early_bufs)

    def right_pass(t, carry):
        d_proj = half_grad(tri_c, t * STEP, sig_b[t], rest_b[t])
        late[:, 0:half] += mm_t(normed_sc[t], d_proj)
        d_normed = mm(w[:, half : 2 * half], d_proj) + d_normed_sc[t]
        sums[0] += fold(d_normed * hat_sc[t], length)
        sums[1] += fold(d_normed, length)
        d_normed_sc[t] = d_normed
        return carry

    lax.fori_loop(0, rows // STEP, right_pass, 0)
    put_stats(late, 0)
    sum_first(1, late, late_bufs)

    def turn_back(values, out, t):
        for r in range(STEP):
            block = mm_t(eye[...], values[:, r * length : (r + 1) * length]).astype(bf16)
            for n, span in enumerate(spans):
                out[t * STEP + r, span, :] = block[n * rows : (n + 1) * rows]

    def last_pass(t, carry):
        hat = hat_sc[t]
        d_hat = d_normed_sc[t] * in_gain[...]
        back = (d_hat - mean_cols(d_hat) - hat * mean_cols(d_hat * hat)) * inv_sc[t]
        turn_back(back.astype(bf16), pair_grad, t)
        return carry

    def update_pass(t, carry):
        turn_back(update_sc[t], update, t)
        return carry

    lax.fori_loop(0, rows // STEP, last_pass, 0)
    copy_out(1).start()
    sum_second(1, late_bufs)
    lax.fori_loop(0, rows // STEP, update_pass, 0)
    copy_out(0).start()
    sum_last(0, early_bufs, (gate_grad, out_grad, proj_grad.at[:, 0:half]), out_norm_grad)
    for n in (3, 4, 6):
        copy_out(n).start()
    sum_third(1, late_bufs)

    for s in range(groups):
        low, high = me - s, me + s

        @pl.when((low >= 0) & (me + 1 < groups))
        def _():
            for c in range(hops):
                hop(act, low, c, right_sem, me + 1).wait_send()

        @pl.when((high < groups) & (me >= 1))
        def _():
            for c in range(hops):
                hop(act, high, c, left_sem, me - 1).wait_send()

    for q in range(cuts):
        for d in range(1, groups):
            col_copy(d, q).wait_send()

    sum_last(1, late_bufs, (proj_grad.at[:, half : 2 * half],), in_norm_grad)
    for n in (2, 5):
        copy_out(n).start()
    for n in range(7):
        copy_out(n).wait()


def finish(count, *refs):
    ins, outs, held, sems = refs[:count], refs[count : 2 * count], refs[2 * count : -1], refs[-1]
    fetch, store = [], []
    for n in range(count):
        fetch.append(pltpu.make_async_copy(ins[n], held[n], sems.at[0, n]))
        store.append(pltpu.make_async_copy(held[n], outs[n], sems.at[1, n]))
    for copy in fetch:
        copy.start()
    for arrived, copy in zip(fetch, store):
        arrived.wait()
        copy.start()
    for copy in store:
        copy.wait()


def shards(
    crops,
    groups,
    pair_act,
    pair_cot,
    in_gain,
    in_bias,
    proj_weight,
    gate_weight,
    out_gain,
    out_bias,
    out_weight,
):
    _, rows, length, channels = pair_act.shape
    hidden = out_weight.shape[0]
    act = pair_act.reshape(rows, length, channels)
    cot = pair_cot.reshape(rows, length, channels)
    anywhere = pl.BlockSpec(memory_space=pl.ANY)
    dma = pltpu.SemaphoreType.DMA
    piece = channels // crops
    cut = min(CUT, rows)
    steps, cells = rows // STEP, STEP * length

    def sum_bufs(width):
        return tuple(pltpu.VMEM((n, piece, width), bf16) for n in (crops, crops, groups, crops))

    def per_step(*shape, dtype=f32):
        return pltpu.VMEM((steps, *shape), dtype)

    early_width, late_width = 3 * channels + 2 * hidden, 2 * hidden + channels
    shapes = (
        jax.ShapeDtypeStruct(act.shape, bf16),
        jax.ShapeDtypeStruct(act.shape, bf16),
        jax.ShapeDtypeStruct(proj_weight.shape, f32),
        jax.ShapeDtypeStruct(gate_weight.shape, f32),
        jax.ShapeDtypeStruct(out_weight.shape, f32),
        jax.ShapeDtypeStruct((2, channels), f32),
        jax.ShapeDtypeStruct((2, hidden), f32),
    )
    results = pl.pallas_call(
        functools.partial(kernel, crops, groups),
        out_shape=shapes,
        in_specs=[anywhere] * 9,
        out_specs=(anywhere,) * 7,
        scratch_shapes=[
            pltpu.VMEM((groups, rows, length, channels), bf16),
            pltpu.VMEM((rows, length, channels), bf16),
            pltpu.VMEM((rows, length, channels), bf16),
            pltpu.VMEM((length, rows, channels), bf16),
            pltpu.VMEM((hidden * cut, length), f32),
            pltpu.VMEM((hidden * cut, length), f32),
            pltpu.VMEM((hidden * cut, length), f32),
            pltpu.VMEM((hidden * cut, length), f32),
            pltpu.VMEM((hidden * length, length), bf16),
            pltpu.VMEM((hidden * length, length), bf16),
            pltpu.VMEM((hidden * rows, length), f32),
            pltpu.VMEM((hidden * rows, length), f32),
            pltpu.VMEM((length * cut, channels), f32),
            per_step(channels, cells, dtype=bf16),
            per_step(channels, cells),
            per_step(1, cells),
            per_step(hidden, cells),
            per_step(hidden, cells),
            per_step(hidden, cells),
            per_step(hidden, cells),
            per_step(channels, cells),
            per_step(channels, cells),
            per_step(hidden, cells),
            per_step(1, cells),
            per_step(channels, cells, dtype=bf16),
            per_step(channels, cells, dtype=bf16),
            per_step(channels, cells, dtype=bf16),
            per_step(channels, cells),
            pltpu.VMEM((4, channels, length), f32),
            dma((9,)),
            dma((groups, rows // STEP)),
            dma((groups, rows // STEP)),
            dma((groups, rows // STEP)),
            dma((groups - 1, rows // cut)),
            dma((groups - 1, rows // cut)),
            pltpu.VMEM((4 * hidden, channels), bf16),
            pltpu.VMEM((channels, channels), bf16),
            pltpu.VMEM((channels, hidden), bf16),
            pltpu.VMEM((channels, channels), bf16),
            pltpu.VMEM((4, channels, 1), f32),
            pltpu.VMEM((channels, early_width), f32),
            pltpu.VMEM((channels, late_width), f32),
            sum_bufs(early_width),
            sum_bufs(late_width),
            dma((2, 2, 2, crops - 1)),
            dma((2, 2, groups - 1)),
            *(pltpu.VMEM(shape.shape, shape.dtype) for shape in shapes),
            dma((7,)),
            pltpu.VMEM((1, channels), f32),
            pltpu.VMEM((1, channels), f32),
            pltpu.VMEM(proj_weight.shape, bf16),
            pltpu.VMEM(gate_weight.shape, bf16),
            pltpu.VMEM((1, hidden), f32),
            pltpu.VMEM((1, hidden), f32),
            pltpu.VMEM(out_weight.shape, bf16),
        ],
        compiler_params=pltpu.CompilerParams(
            collective_id=0, has_side_effects=True, vmem_limit_bytes=60 * 1024 * 1024
        ),
        name="tri",
    )(
        act,
        cot,
        in_gain.reshape(1, channels),
        in_bias.reshape(1, channels),
        proj_weight,
        gate_weight,
        out_gain.reshape(1, hidden),
        out_bias.reshape(1, hidden),
        out_weight,
    )
    update, pair_grad, *grads = pl.pallas_call(
        functools.partial(finish, 7),
        out_shape=shapes,
        in_specs=[anywhere] * 7,
        out_specs=(anywhere,) * 7,
        scratch_shapes=[*(pltpu.VMEM(shape.shape, shape.dtype) for shape in shapes), dma((2, 7))],
        name="finish",
    )(*results)
    return (update.reshape(pair_act.shape), pair_grad.reshape(pair_act.shape), *grads)


def solution(mesh):
    placed = (P("dp", "dap", None, None),) * 2 + (P(),) * 7
    return jax.shard_map(
        functools.partial(shards, mesh.shape["dp"], mesh.shape["dap"]),
        mesh=mesh,
        in_specs=placed,
        out_specs=(P("dp", "dap", None, None), P("dp", "dap", None, None), P(), P(), P(), P(), P()),
        check_vma=False,
    )
```

```python
import functools

import jax
import jax.numpy as jnp
from jax import lax
from jax.experimental import pallas as pl
from jax.experimental.pallas import tpu as pltpu
from jax.sharding import PartitionSpec as P

epsilon = 1e-05
f32 = jnp.float32
bf16 = jnp.bfloat16
STEP = 8
CUT = 16


def mm(a, b):
    return jnp.dot(a, b, preferred_element_type=f32)


def mm_t(a, b):
    return lax.dot_general(a, b, (((1,), (1,)), ((), ())), preferred_element_type=f32)


def sigmoid(v):
    return 0.5 * jnp.tanh(0.5 * v) + 0.5


def norm_cols(values):
    count = values.shape[0]
    centred = values - jnp.sum(values, axis=0, keepdims=True) * (1.0 / count)
    var = jnp.sum(centred * centred, axis=0, keepdims=True) * (1.0 / count)
    inv_std = lax.rsqrt(var + epsilon)
    return centred * inv_std, inv_std


def mean_cols(values):
    return jnp.sum(values, axis=0, keepdims=True) * (1.0 / values.shape[0])


def fold(values, width):
    total = values[:, 0:width]
    for at in range(width, values.shape[1], width):
        total = total + values[:, at : at + width]
    return total


def kernel(
    crops,
    groups,
    act,
    cot_arg,
    in_gain_arg,
    in_bias_arg,
    w_arg,
    wg_arg,
    out_gain_arg,
    out_bias_arg,
    wo_arg,
    update_out,
    pair_grad_out,
    proj_grad_out,
    gate_grad_out,
    out_grad_out,
    in_norm_grad_out,
    out_norm_grad_out,
    act_all,
    cot,
    mixed_grad,
    mixed_cols,
    left_part,
    right_part,
    left_high,
    right_high,
    left,
    right,
    tri_r,
    tri_c,
    col_grad,
    normed_sc,
    hat_sc,
    inv_sc,
    sig_a,
    rest_a,
    sig_b,
    rest_b,
    gate_sc,
    slope_sc,
    d_out_sc,
    first_sc,
    d_mixed_sc,
    update_sc,
    d_gate_sc,
    d_normed_sc,
    sums,
    in_sems,
    recv_sem,
    right_sem,
    left_sem,
    col_send,
    col_recv,
    w_t,
    wg_t,
    wo_t,
    eye,
    columns,
    early,
    late,
    early_bufs,
    late_bufs,
    sum_sems,
    swap_sems,
    update,
    pair_grad,
    proj_grad,
    gate_grad,
    out_grad,
    in_norm_grad,
    out_norm_grad,
    out_sems,
    in_gain_row,
    in_bias_row,
    w,
    wg,
    out_gain_row,
    out_bias_row,
    wo,
):
    me = lax.axis_index("dap")
    crop = lax.axis_index("dp")
    rows, length, channels = act.shape
    hidden = wo.shape[0]
    cut = min(CUT, rows)
    cuts = rows // cut
    cells = STEP * length
    hops = rows // STEP
    wide = length // 2
    near = jnp.minimum(me, groups - 1 - me)

    def block_in(slot):
        if slot == 0:
            return me
        step = (slot + 1) // 2
        paired = me - step if slot % 2 else me + step
        alone = jnp.where(me == near, me + slot - near, me - slot + near)
        return jnp.where(slot <= 2 * near, paired, alone)

    def slot_of(block):
        step = jnp.abs(block - me)
        paired = jnp.where(block < me, 2 * step - 1, 2 * step)
        return jnp.where(step <= near, paired, near + step)

    spans = [pl.ds(pl.multiple_of(block_in(n) * rows, rows), rows) for n in range(groups)]

    def cells_of(ref, first):
        part = pl.ds(first, STEP)
        return jnp.concatenate([ref[part, span, :] for span in spans], axis=1).reshape(
            cells, channels
        )

    per_cut = cut // STEP
    pair, pair_cut = min(2, rows // STEP), min(2, cut // STEP)
    parts = ((left_part, right_part), (left_high, right_high))

    act_in = pltpu.make_async_copy(act, act_all.at[me], in_sems.at[0])
    cot_in = pltpu.make_async_copy(cot_arg, cot, in_sems.at[1])
    results = (
        (update, update_out),
        (pair_grad, pair_grad_out),
        (proj_grad, proj_grad_out),
        (gate_grad, gate_grad_out),
        (out_grad, out_grad_out),
        (in_norm_grad, in_norm_grad_out),
        (out_norm_grad, out_norm_grad_out),
    )

    def copy_out(n):
        return pltpu.make_async_copy(*results[n], out_sems.at[n])

    small_in = [
        pltpu.make_async_copy(src, dst, in_sems.at[2 + n])
        for n, (src, dst) in enumerate(
            (
                (w_arg, w),
                (wg_arg, wg),
                (wo_arg, wo),
                (in_gain_arg, in_gain_row),
                (in_bias_arg, in_bias_row),
                (out_gain_arg, out_gain_row),
                (out_bias_arg, out_bias_row),
            )
        )
    ]
    act_in.start()
    for copy in small_in:
        copy.start()
    cot_in.start()

    barrier = pltpu.get_barrier_semaphore()
    for d in range(1, groups):
        pl.semaphore_signal(
            barrier,
            inc=1,
            device_id={"dap": lax.rem(me + d, groups)},
            device_id_type=pl.DeviceIdType.MESH,
        )
    for d in range(1, crops):
        pl.semaphore_signal(
            barrier,
            inc=1,
            device_id={"dp": lax.rem(crop + d, crops)},
            device_id_type=pl.DeviceIdType.MESH,
        )
    pl.semaphore_wait(barrier, groups + crops - 2)

    def hop(src, block, c, send_sems, to):
        part = pl.ds(c * STEP, STEP)
        return pltpu.make_async_remote_copy(
            src_ref=src.at[part],
            dst_ref=act_all.at[block, part],
            send_sem=send_sems.at[block, c],
            recv_sem=recv_sem.at[block, c],
            device_id={"dap": to},
            device_id_type=pl.DeviceIdType.MESH,
        )

    def col_copy(d, q):
        peer = lax.rem(me + d, groups)
        at = pl.multiple_of(slot_of(peer) * rows + q * cut, cut)
        mine = pl.multiple_of(me * rows, rows)
        return pltpu.make_async_remote_copy(
            src_ref=mixed_grad.at[:, pl.ds(at, cut), :],
            dst_ref=mixed_cols.at[pl.ds(mine, rows), pl.ds(q * cut, cut), :],
            send_sem=col_send.at[d - 1, q],
            recv_sem=col_recv.at[d - 1, q],
            device_id={"dap": peer},
            device_id_type=pl.DeviceIdType.MESH,
        )

    @pl.when(me + 1 < groups)
    def _():
        for c in range(hops):
            hop(act, me, c, right_sem, me + 1).start()

    @pl.when(me >= 1)
    def _():
        for c in range(hops):
            hop(act, me, c, left_sem, me - 1).start()

    for copy in small_in:
        copy.wait()

    def turned(block):
        return jnp.transpose(block.astype(f32)).astype(bf16)

    for n in range(4):
        w_t[n * hidden : (n + 1) * hidden, :] = turned(w[:, n * hidden : (n + 1) * hidden])
    wg_t[...] = turned(wg[...])
    wo_t[...] = turned(wo[...])
    square = (channels, channels)
    eye[...] = (
        (lax.broadcasted_iota(jnp.int32, square, 0) == lax.broadcasted_iota(jnp.int32, square, 1))
        .astype(f32)
        .astype(bf16)
    )
    for n, row in enumerate((in_gain_row, in_bias_row, out_gain_row, out_bias_row)):
        columns[n] = jnp.transpose(jnp.broadcast_to(row[...], square))[:, 0:1]
    in_gain, in_bias, out_gain, out_bias = (columns.at[n] for n in range(4))
    sums[...] = jnp.zeros_like(sums)
    early[...] = jnp.zeros_like(early)
    late[...] = jnp.zeros_like(late)

    def piece_copy(which, stage, bufs, e):
        peer = lax.rem(crop + e, crops)
        sent, got, _, total = bufs
        src, dst = (sent.at[peer], got.at[crop]) if stage == 0 else (total.at[crop],) * 2
        return pltpu.make_async_remote_copy(
            src_ref=src,
            dst_ref=dst,
            send_sem=sum_sems.at[which, stage, 0, e - 1],
            recv_sem=sum_sems.at[which, stage, 1, e - 1],
            device_id={"dp": peer},
            device_id_type=pl.DeviceIdType.MESH,
        )

    def swap_copy(which, bufs, d):
        part = bufs[2]
        return pltpu.make_async_remote_copy(
            src_ref=part.at[me],
            dst_ref=part.at[me],
            send_sem=swap_sems.at[which, 0, d - 1],
            recv_sem=swap_sems.at[which, 1, d - 1],
            device_id={"dap": lax.rem(me + d, groups)},
            device_id_type=pl.DeviceIdType.MESH,
        )

    piece = channels // crops

    def sum_first(which, acc, bufs):
        for p in range(crops):
            bufs[0][p] = acc[p * piece : (p + 1) * piece, :].astype(bf16)
        for e in range(1, crops):
            piece_copy(which, 0, bufs, e).start()

    def sum_second(which, bufs):
        total = bufs[0][crop].astype(f32)
        for e in range(1, crops):
            piece_copy(which, 0, bufs, e).wait_recv()
            total = total + bufs[1][lax.rem(crop + crops - e, crops)]
        bufs[2][me] = total.astype(bf16)
        for d in range(1, groups):
            swap_copy(which, bufs, d).start()

    def sum_third(which, bufs):
        for d in range(1, groups):
            swap_copy(which, bufs, d).wait_recv()
        total = bufs[2][0].astype(f32)
        for g in range(1, groups):
            total = total + bufs[2][g]
        bufs[3][crop] = (total * (1.0 / length)).astype(bf16)
        for e in range(1, crops):
            piece_copy(which, 1, bufs, e).start()

    def sum_last(which, bufs, outs, stats_out):
        for e in range(1, crops):
            piece_copy(which, 1, bufs, e).wait_recv()
        total = jnp.concatenate([bufs[3][p] for p in range(crops)], axis=0).astype(f32)
        at = 0
        for out in outs:
            out[...] = total[:, at : at + out.shape[1]]
            at += out.shape[1]
        turned_stats = jnp.transpose(total[:, at : at + channels])
        stats_out[0:1, :] = turned_stats[0:1]
        stats_out[1:2, :] = turned_stats[8:9]
        for e in range(1, crops):
            piece_copy(which, 0, bufs, e).wait_send()
            piece_copy(which, 1, bufs, e).wait_send()
        for d in range(1, groups):
            swap_copy(which, bufs, d).wait_send()

    def put_stats(acc, first):
        at = acc.shape[1] - channels
        for n in range(2):
            acc[:, at + 8 * n : at + 8 * n + 8] = jnp.broadcast_to(
                jnp.sum(sums[first + n], axis=1, keepdims=True), (channels, 8)
            )

    def normed_of(x):
        hat, inv = norm_cols(mm_t(eye[...], x))
        return hat, inv, (hat * in_gain[...] + in_bias[...]).astype(bf16)

    def put_part(ref, first, values):
        for r in range(STEP):
            ref[pl.ds(first + r, hidden, stride=cut), :] = values[:, r * length : (r + 1) * length]

    def settle(side, base):
        left_part, right_part = parts[side]

        def body(h, carry):
            frm = pl.ds(pl.multiple_of(h * cut, cut), cut)
            to = pl.ds(pl.multiple_of(h * length + base, cut), cut)
            left[to, :] = left_part[frm, :].astype(bf16)
            right[to, :] = right_part[frm, :].astype(bf16)
            return carry

        lax.fori_loop(0, hidden, body, 0, unroll=8)

    def sides(side, block, c):
        left_part, right_part = parts[side]
        x = cells_of(act_all.at[block], c * STEP)
        _, _, normed = normed_of(x)
        pj = mm(w_t[...], normed)
        first = c % per_cut * STEP
        put_part(left_part, first, sigmoid(pj[0:hidden]) * pj[hidden : 2 * hidden])
        put_part(
            right_part, first, sigmoid(pj[2 * hidden : 3 * hidden]) * pj[3 * hidden : 4 * hidden]
        )
        if c % per_cut == per_cut - 1:
            settle(side, slot_of(block) * rows + c // per_cut * cut)

    def own_sides(c):
        left_part, right_part = parts[0]

        def body(t, carry):
            at = c * (cut // STEP) + t
            x = cells_of(act_all.at[me], at * STEP)
            hat, inv, normed = normed_of(x)
            hat_sc[at] = hat
            inv_sc[at] = inv
            normed_sc[at] = normed
            pj = mm(w_t[...], normed)
            sa, va = sigmoid(pj[0:hidden]), pj[hidden : 2 * hidden]
            sig_a[at] = sa
            rest_a[at] = va * (1.0 - sa)
            put_part(left_part, t * STEP, sa * va)
            sb, vb = sigmoid(pj[2 * hidden : 3 * hidden]), pj[3 * hidden : 4 * hidden]
            sig_b[at] = sb
            rest_b[at] = vb * (1.0 - sb)
            put_part(right_part, t * STEP, sb * vb)
            return carry

        lax.fori_loop(0, cut // STEP, body, 0)
        settle(0, c * cut)

    def own_gate(t, carry):
        gate = sigmoid(mm(wg_t[...], normed_sc[t]))
        cot_t = mm_t(eye[...], cells_of(cot, t * STEP))
        grad = cot_t * gate
        gate_sc[t] = gate
        slope_sc[t] = grad * (1.0 - gate)
        d_mixed = grad.astype(bf16)
        d_mixed_sc[t] = d_mixed
        for r in range(STEP):
            mixed_grad[t * STEP + r] = mm_t(
                eye[...], d_mixed[:, r * length : (r + 1) * length]
            ).astype(bf16)
        d_out = mm(wo[...], d_mixed)
        d_out_sc[t] = d_out
        first_sc[t] = mean_cols(d_out * out_gain[...])
        sums[3] += fold(d_out, length)
        return carry

    def at_end(device):
        return (device == 0) | (device == groups - 1)

    def send_cols(from_end, to_end):
        for q in range(cuts):
            for d in range(1, groups):
                peer_at_end = at_end(lax.rem(me + d, groups))

                @pl.when((at_end(me) == from_end) & (peer_at_end == to_end))
                def _():
                    col_copy(d, q).start()

    act_in.wait()
    for c in range(cuts):
        own_sides(c)
    cot_in.wait()
    lax.fori_loop(0, rows // STEP, own_gate, 0)

    def products(late_half):
        def body(h, carry):
            at = h * length
            half_rows = pl.ds(pl.multiple_of(at + late_half * wide, wide), wide)
            own = pl.ds(pl.multiple_of(at, rows), rows)
            to = pl.ds(pl.multiple_of(h * rows, rows), rows)
            sides_of = [right[half_rows, :], left[half_rows, :]]
            both = mm_t(
                jnp.concatenate([left[own, :], right[own, :]], axis=0),
                jnp.concatenate(sides_of[::-1] if late_half else sides_of, axis=0),
            )
            row_lanes = slice(wide, length) if late_half else slice(0, wide)
            col_lanes = slice(0, wide) if late_half else slice(wide, length)
            tri_r[to, row_lanes] = both[0:rows, row_lanes]
            tri_c[to, col_lanes] = both[rows : 2 * rows, col_lanes]
            return carry

        lax.fori_loop(0, hidden, body, 0, unroll=16)

    for s in range(1, groups):
        low, high = me - s, me + s
        for c in range(hops):

            @pl.when(low >= 0)
            def _():
                hop(act, low, c, right_sem, me).wait_recv()

                @pl.when(me + 1 < groups)
                def _():
                    hop(act_all.at[low], low, c, right_sem, me + 1).start()

            @pl.when(high < groups)
            def _():
                hop(act, high, c, left_sem, me).wait_recv()

                @pl.when(me >= 1)
                def _():
                    hop(act_all.at[high], high, c, left_sem, me - 1).start()

            if s == groups - 1 and c == hops - 1:
                send_cols(True, True)
                send_cols(True, False)
                send_cols(False, False)
                send_cols(False, True)

            @pl.when(low >= 0)
            def _():
                sides(0, low, c)

            @pl.when(high < groups)
            def _():
                sides(1, high, c)

        if s == max(1, groups // 2):
            products(0)

    products(1)

    def slabs(ref, first):
        return jnp.concatenate(
            [ref[pl.ds(first + r, hidden, stride=rows), :] for r in range(STEP)], axis=1
        )

    def put_slabs(ref, first, values):
        for r in range(STEP):
            ref[pl.ds(first + r, hidden, stride=rows), :] = values[
                :, r * length : (r + 1) * length
            ]

    def row_pass(t, carry):
        first = t * STEP
        hat, inv = norm_cols(slabs(tri_r, first).astype(bf16).astype(f32))
        tri_norm = (hat * out_gain[...] + out_bias[...]).astype(bf16)
        d_out = d_out_sc[t]
        scaled = d_out * hat
        sums[2] += fold(scaled, length)
        second = mean_cols(scaled * out_gain[...])
        put_slabs(tri_r, first, (d_out * out_gain[...] - first_sc[t] - hat * second) * inv)
        mixed = mm(wo_t[...], tri_norm)
        update_sc[t] = (gate_sc[t] * mixed).astype(bf16)
        d_gate = (slope_sc[t] * mixed).astype(bf16)
        d_gate_sc[t] = d_gate
        early[:, 0:channels] += mm_t(normed_sc[t], d_gate)
        early[:, channels : 2 * channels] += mm_t(tri_norm, d_mixed_sc[t])
        return carry

    lax.fori_loop(0, rows // STEP, row_pass, 0, unroll=pair)

    def back_rows(h, carry):
        r_all = right[pl.ds(pl.multiple_of(h * length, length), length), :]
        to = pl.ds(pl.multiple_of(h * rows, rows), rows)
        tri_r[to, :] = mm(tri_r[to, :].astype(bf16), r_all)
        return carry

    lax.fori_loop(0, hidden, back_rows, 0, unroll=16)

    half = 2 * hidden

    def half_grad(ref, first, sig, rest):
        d_val = slabs(ref, first).astype(bf16).astype(f32) * sig
        return jnp.concatenate([(d_val * rest).astype(bf16), d_val.astype(bf16)], axis=0)

    def left_pass(t, carry):
        d_proj = half_grad(tri_r, t * STEP, sig_a[t], rest_a[t])
        early[:, 2 * channels : 2 * channels + half] += mm_t(normed_sc[t], d_proj)
        d_normed_sc[t] = mm(w[:, 0:half], d_proj) + mm(wg[...], d_gate_sc[t])
        return carry

    lax.fori_loop(0, rows // STEP, left_pass, 0, unroll=pair)
    put_stats(early, 2)
    sum_first(0, early, early_bufs)

    hat_c, inv_c = d_out_sc, first_sc

    def col_norm(t, carry):
        hat_c[t], inv_c[t] = norm_cols(slabs(tri_c, t * STEP).astype(bf16).astype(f32))
        return carry

    lax.fori_loop(0, rows // STEP, col_norm, 0, unroll=pair)

    def columns_of(ref, first):
        return jnp.concatenate(
            [ref[pl.ds(first + r, length, stride=cut), :] for r in range(STEP)], axis=0
        ).astype(bf16)

    for q in range(cuts):

        def unpack_own(t, carry):
            to = pl.ds(pl.multiple_of((wide + t) * cut, cut), cut)
            col_grad[to, :] = mixed_grad[t, q * cut : q * cut + cut, :].astype(f32)
            return carry

        lax.fori_loop(0, rows, unpack_own, 0, unroll=4)
        for d in range(1, groups):
            col_copy(d, q).wait_recv()
        for d in range(1, groups):
            peer = lax.rem(me + d, groups)

            at = lax.rem(slot_of(peer) * rows + wide, length)

            def unpack_peer(t, carry):
                to = pl.ds(pl.multiple_of((at + t) * cut, cut), cut)
                col_grad[to, :] = mixed_cols[peer * rows + t, q * cut : q * cut + cut, :].astype(f32)
                return carry

            lax.fori_loop(0, rows, unpack_peer, 0, unroll=4)

        def col_pass(t, carry):
            at = q * (cut // STEP) + t
            hat = hat_c[at]
            d_hat = mm_t(wo[...], columns_of(col_grad, t * STEP)) * out_gain[...]
            back = (d_hat - mean_cols(d_hat) - hat * mean_cols(d_hat * hat)) * inv_c[at]
            put_slabs(tri_c, at * STEP, back)
            return carry

        lax.fori_loop(0, cut // STEP, col_pass, 0, unroll=pair_cut)

    sum_second(0, early_bufs)

    def back_cols(h, carry):
        at = h * length
        l_all = jnp.concatenate(
            [left[pl.ds(pl.multiple_of(at + n * wide, wide), wide), :] for n in (1, 0)], axis=0
        )
        to = pl.ds(pl.multiple_of(h * rows, rows), rows)
        tri_c[to, :] = mm(tri_c[to, :].astype(bf16), l_all)
        return carry

    lax.fori_loop(0, hidden, back_cols, 0, unroll=16)
    sum_third(0, early_bufs)

    def right_pass(t, carry):
        d_proj = half_grad(tri_c, t * STEP, sig_b[t], rest_b[t])
        late[:, 0:half] += mm_t(normed_sc[t], d_proj)
        d_normed = mm(w[:, half : 2 * half], d_proj) + d_normed_sc[t]
        sums[0] += fold(d_normed * hat_sc[t], length)
        sums[1] += fold(d_normed, length)
        d_normed_sc[t] = d_normed
        return carry

    lax.fori_loop(0, rows // STEP, right_pass, 0, unroll=pair)
    put_stats(late, 0)
    sum_first(1, late, late_bufs)

    def turn_back(values, out, t):
        for r in range(STEP):
            block = mm_t(eye[...], values[:, r * length : (r + 1) * length]).astype(bf16)
            for n, span in enumerate(spans):
                out[t * STEP + r, span, :] = block[n * rows : (n + 1) * rows]

    def last_pass(t, carry):
        hat = hat_sc[t]
        d_hat = d_normed_sc[t] * in_gain[...]
        back = (d_hat - mean_cols(d_hat) - hat * mean_cols(d_hat * hat)) * inv_sc[t]
        turn_back(back.astype(bf16), pair_grad, t)
        return carry

    def update_pass(t, carry):
        turn_back(update_sc[t], update, t)
        return carry

    lax.fori_loop(0, rows // STEP, last_pass, 0, unroll=pair)
    copy_out(1).start()
    sum_second(1, late_bufs)
    lax.fori_loop(0, rows // STEP, update_pass, 0, unroll=pair)
    copy_out(0).start()
    sum_last(0, early_bufs, (gate_grad, out_grad, proj_grad.at[:, 0:half]), out_norm_grad)
    for n in (3, 4, 6):
        copy_out(n).start()
    sum_third(1, late_bufs)

    for s in range(groups):
        low, high = me - s, me + s

        @pl.when((low >= 0) & (me + 1 < groups))
        def _():
            for c in range(hops):
                hop(act, low, c, right_sem, me + 1).wait_send()

        @pl.when((high < groups) & (me >= 1))
        def _():
            for c in range(hops):
                hop(act, high, c, left_sem, me - 1).wait_send()

    for q in range(cuts):
        for d in range(1, groups):
            col_copy(d, q).wait_send()

    sum_last(1, late_bufs, (proj_grad.at[:, half : 2 * half],), in_norm_grad)
    for n in (2, 5):
        copy_out(n).start()
    for n in range(7):
        copy_out(n).wait()


def finish(count, *refs):
    ins, outs, held, sems = refs[:count], refs[count : 2 * count], refs[2 * count : -1], refs[-1]
    fetch, store = [], []
    for n in range(count):
        fetch.append(pltpu.make_async_copy(ins[n], held[n], sems.at[0, n]))
        store.append(pltpu.make_async_copy(held[n], outs[n], sems.at[1, n]))
    for copy in fetch:
        copy.start()
    for arrived, copy in zip(fetch, store):
        arrived.wait()
        copy.start()
    for copy in store:
        copy.wait()


def shards(
    crops,
    groups,
    pair_act,
    pair_cot,
    in_gain,
    in_bias,
    proj_weight,
    gate_weight,
    out_gain,
    out_bias,
    out_weight,
):
    _, rows, length, channels = pair_act.shape
    hidden = out_weight.shape[0]
    act = pair_act.reshape(rows, length, channels)
    cot = pair_cot.reshape(rows, length, channels)
    anywhere = pl.BlockSpec(memory_space=pl.ANY)
    dma = pltpu.SemaphoreType.DMA
    piece = channels // crops
    cut = min(CUT, rows)
    steps, cells = rows // STEP, STEP * length

    def sum_bufs(width):
        return tuple(pltpu.VMEM((n, piece, width), bf16) for n in (crops, crops, groups, crops))

    def per_step(*shape, dtype=f32):
        return pltpu.VMEM((steps, *shape), dtype)

    early_width, late_width = 3 * channels + 2 * hidden, 2 * hidden + channels
    shapes = (
        jax.ShapeDtypeStruct(act.shape, bf16),
        jax.ShapeDtypeStruct(act.shape, bf16),
        jax.ShapeDtypeStruct(proj_weight.shape, f32),
        jax.ShapeDtypeStruct(gate_weight.shape, f32),
        jax.ShapeDtypeStruct(out_weight.shape, f32),
        jax.ShapeDtypeStruct((2, channels), f32),
        jax.ShapeDtypeStruct((2, hidden), f32),
    )
    results = pl.pallas_call(
        functools.partial(kernel, crops, groups),
        out_shape=shapes,
        in_specs=[anywhere] * 9,
        out_specs=(anywhere,) * 7,
        scratch_shapes=[
            pltpu.VMEM((groups, rows, length, channels), bf16),
            pltpu.VMEM((rows, length, channels), bf16),
            pltpu.VMEM((rows, length, channels), bf16),
            pltpu.VMEM((length, rows, channels), bf16),
            pltpu.VMEM((hidden * cut, length), f32),
            pltpu.VMEM((hidden * cut, length), f32),
            pltpu.VMEM((hidden * cut, length), f32),
            pltpu.VMEM((hidden * cut, length), f32),
            pltpu.VMEM((hidden * length, length), bf16),
            pltpu.VMEM((hidden * length, length), bf16),
            pltpu.VMEM((hidden * rows, length), f32),
            pltpu.VMEM((hidden * rows, length), f32),
            pltpu.VMEM((length * cut, channels), f32),
            per_step(channels, cells, dtype=bf16),
            per_step(channels, cells),
            per_step(1, cells),
            per_step(hidden, cells),
            per_step(hidden, cells),
            per_step(hidden, cells),
            per_step(hidden, cells),
            per_step(channels, cells),
            per_step(channels, cells),
            per_step(hidden, cells),
            per_step(1, cells),
            per_step(channels, cells, dtype=bf16),
            per_step(channels, cells, dtype=bf16),
            per_step(channels, cells, dtype=bf16),
            per_step(channels, cells),
            pltpu.VMEM((4, channels, length), f32),
            dma((9,)),
            dma((groups, rows // STEP)),
            dma((groups, rows // STEP)),
            dma((groups, rows // STEP)),
            dma((groups - 1, rows // cut)),
            dma((groups - 1, rows // cut)),
            pltpu.VMEM((4 * hidden, channels), bf16),
            pltpu.VMEM((channels, channels), bf16),
            pltpu.VMEM((channels, hidden), bf16),
            pltpu.VMEM((channels, channels), bf16),
            pltpu.VMEM((4, channels, 1), f32),
            pltpu.VMEM((channels, early_width), f32),
            pltpu.VMEM((channels, late_width), f32),
            sum_bufs(early_width),
            sum_bufs(late_width),
            dma((2, 2, 2, crops - 1)),
            dma((2, 2, groups - 1)),
            *(pltpu.VMEM(shape.shape, shape.dtype) for shape in shapes),
            dma((7,)),
            pltpu.VMEM((1, channels), f32),
            pltpu.VMEM((1, channels), f32),
            pltpu.VMEM(proj_weight.shape, bf16),
            pltpu.VMEM(gate_weight.shape, bf16),
            pltpu.VMEM((1, hidden), f32),
            pltpu.VMEM((1, hidden), f32),
            pltpu.VMEM(out_weight.shape, bf16),
        ],
        compiler_params=pltpu.CompilerParams(
            collective_id=0, has_side_effects=True, vmem_limit_bytes=60 * 1024 * 1024
        ),
        name="tri",
    )(
        act,
        cot,
        in_gain.reshape(1, channels),
        in_bias.reshape(1, channels),
        proj_weight,
        gate_weight,
        out_gain.reshape(1, hidden),
        out_bias.reshape(1, hidden),
        out_weight,
    )
    update, pair_grad, *grads = pl.pallas_call(
        functools.partial(finish, 7),
        out_shape=shapes,
        in_specs=[anywhere] * 7,
        out_specs=(anywhere,) * 7,
        scratch_shapes=[*(pltpu.VMEM(shape.shape, shape.dtype) for shape in shapes), dma((2, 7))],
        name="finish",
    )(*results)
    return (update.reshape(pair_act.shape), pair_grad.reshape(pair_act.shape), *grads)


def solution(mesh):
    placed = (P("dp", "dap", None, None),) * 2 + (P(),) * 7
    return jax.shard_map(
        functools.partial(shards, mesh.shape["dp"], mesh.shape["dap"]),
        mesh=mesh,
        in_specs=placed,
        out_specs=(P("dp", "dap", None, None), P("dp", "dap", None, None), P(), P(), P(), P(), P()),
        check_vma=False,
    )
```

```python
import functools

import jax
import jax.numpy as jnp
from jax import lax
from jax.experimental import pallas as pl
from jax.experimental.pallas import tpu as pltpu
from jax.sharding import PartitionSpec as P

epsilon = 1e-05
f32 = jnp.float32
bf16 = jnp.bfloat16
STEP = 8
CUT = 16
PARTS = 4


def mm(a, b):
    return jnp.dot(a, b, preferred_element_type=f32)


def mm_t(a, b):
    return lax.dot_general(a, b, (((1,), (1,)), ((), ())), preferred_element_type=f32)


def sigmoid(v):
    return 0.5 * jnp.tanh(0.5 * v) + 0.5


def norm_cols(values):
    count = values.shape[0]
    centred = values - jnp.sum(values, axis=0, keepdims=True) * (1.0 / count)
    var = jnp.sum(centred * centred, axis=0, keepdims=True) * (1.0 / count)
    inv_std = lax.rsqrt(var + epsilon)
    return centred * inv_std, inv_std


def mean_cols(values):
    return jnp.sum(values, axis=0, keepdims=True) * (1.0 / values.shape[0])


def fold(values, width):
    total = values[:, 0:width]
    for at in range(width, values.shape[1], width):
        total = total + values[:, at : at + width]
    return total


def kernel(
    crops,
    groups,
    act,
    cot_arg,
    in_gain_arg,
    in_bias_arg,
    w_arg,
    wg_arg,
    out_gain_arg,
    out_bias_arg,
    wo_arg,
    update_out,
    pair_grad_out,
    proj_grad_out,
    gate_grad_out,
    out_grad_out,
    in_norm_grad_out,
    out_norm_grad_out,
    act_all,
    cot,
    mixed_grad,
    mixed_cols,
    left_part,
    right_part,
    left_high,
    right_high,
    left,
    right,
    tri_r,
    tri_c,
    col_grad,
    normed_sc,
    hat_sc,
    inv_sc,
    sig_a,
    rest_a,
    sig_b,
    rest_b,
    gate_sc,
    slope_sc,
    d_out_sc,
    first_sc,
    d_mixed_sc,
    update_sc,
    d_gate_sc,
    d_normed_sc,
    sums,
    in_sems,
    recv_sem,
    right_sem,
    left_sem,
    col_send,
    col_recv,
    w_t,
    wg_t,
    wo_t,
    eye,
    columns,
    early,
    late,
    early_bufs,
    late_bufs,
    sum_sems,
    swap_sems,
    update,
    pair_grad,
    proj_grad,
    gate_grad,
    out_grad,
    in_norm_grad,
    out_norm_grad,
    out_sems,
    in_gain_row,
    in_bias_row,
    w,
    wg,
    out_gain_row,
    out_bias_row,
    wo,
):
    me = lax.axis_index("dap")
    crop = lax.axis_index("dp")
    rows, length, channels = act.shape
    hidden = wo.shape[0]
    cut = min(CUT, rows)
    cuts = rows // cut
    cells = STEP * length
    hops = rows // STEP
    wide = length // 2
    near = jnp.minimum(me, groups - 1 - me)

    def block_in(slot):
        if slot == 0:
            return me
        step = (slot + 1) // 2
        paired = me - step if slot % 2 else me + step
        alone = jnp.where(me == near, me + slot - near, me - slot + near)
        return jnp.where(slot <= 2 * near, paired, alone)

    def slot_of(block):
        step = jnp.abs(block - me)
        paired = jnp.where(block < me, 2 * step - 1, 2 * step)
        return jnp.where(step <= near, paired, near + step)

    spans = [pl.ds(pl.multiple_of(block_in(n) * rows, rows), rows) for n in range(groups)]

    def cells_of(ref, first):
        part = pl.ds(first, STEP)
        return jnp.concatenate([ref[part, span, :] for span in spans], axis=1).reshape(
            cells, channels
        )

    per_cut = cut // STEP
    pair, pair_cut = min(2, rows // STEP), min(2, cut // STEP)
    parts = ((left_part, right_part), (left_high, right_high))

    act_in = pltpu.make_async_copy(act, act_all.at[me], in_sems.at[0])
    cot_in = pltpu.make_async_copy(cot_arg, cot, in_sems.at[1])
    results = (
        (update, update_out),
        (pair_grad, pair_grad_out),
        (proj_grad, proj_grad_out),
        (gate_grad, gate_grad_out),
        (out_grad, out_grad_out),
        (in_norm_grad, in_norm_grad_out),
        (out_norm_grad, out_norm_grad_out),
    )

    def copy_out(n):
        return pltpu.make_async_copy(*results[n], out_sems.at[n])

    small_in = [
        pltpu.make_async_copy(src, dst, in_sems.at[2 + n])
        for n, (src, dst) in enumerate(
            (
                (w_arg, w),
                (wg_arg, wg),
                (wo_arg, wo),
                (in_gain_arg, in_gain_row),
                (in_bias_arg, in_bias_row),
                (out_gain_arg, out_gain_row),
                (out_bias_arg, out_bias_row),
            )
        )
    ]
    act_in.start()
    for copy in small_in:
        copy.start()
    cot_in.start()

    barrier = pltpu.get_barrier_semaphore()
    for d in range(1, groups):
        pl.semaphore_signal(
            barrier,
            inc=1,
            device_id={"dap": lax.rem(me + d, groups)},
            device_id_type=pl.DeviceIdType.MESH,
        )
    for d in range(1, crops):
        pl.semaphore_signal(
            barrier,
            inc=1,
            device_id={"dp": lax.rem(crop + d, crops)},
            device_id_type=pl.DeviceIdType.MESH,
        )
    pl.semaphore_wait(barrier, groups + crops - 2)

    def hop(src, block, c, send_sems, to):
        part = pl.ds(c * STEP, STEP)
        return pltpu.make_async_remote_copy(
            src_ref=src.at[part],
            dst_ref=act_all.at[block, part],
            send_sem=send_sems.at[block, c],
            recv_sem=recv_sem.at[block, c],
            device_id={"dap": to},
            device_id_type=pl.DeviceIdType.MESH,
        )

    def col_copy(d, q):
        peer = lax.rem(me + d, groups)
        at = pl.multiple_of(slot_of(peer) * rows + q * cut, cut)
        mine = pl.multiple_of(me * rows, rows)
        return pltpu.make_async_remote_copy(
            src_ref=mixed_grad.at[:, pl.ds(at, cut), :],
            dst_ref=mixed_cols.at[pl.ds(mine, rows), pl.ds(q * cut, cut), :],
            send_sem=col_send.at[d - 1, q],
            recv_sem=col_recv.at[d - 1, q],
            device_id={"dap": peer},
            device_id_type=pl.DeviceIdType.MESH,
        )

    @pl.when(me + 1 < groups)
    def _():
        for c in range(hops):
            hop(act, me, c, right_sem, me + 1).start()

    @pl.when(me >= 1)
    def _():
        for c in range(hops):
            hop(act, me, c, left_sem, me - 1).start()

    for copy in small_in:
        copy.wait()

    def turned(block):
        return jnp.transpose(block.astype(f32)).astype(bf16)

    for n in range(4):
        w_t[n * hidden : (n + 1) * hidden, :] = turned(w[:, n * hidden : (n + 1) * hidden])
    wg_t[...] = turned(wg[...])
    wo_t[...] = turned(wo[...])
    square = (channels, channels)
    eye[...] = (
        (lax.broadcasted_iota(jnp.int32, square, 0) == lax.broadcasted_iota(jnp.int32, square, 1))
        .astype(f32)
        .astype(bf16)
    )
    for n, row in enumerate((in_gain_row, in_bias_row, out_gain_row, out_bias_row)):
        columns[n] = jnp.transpose(jnp.broadcast_to(row[...], square))[:, 0:1]
    in_gain, in_bias, out_gain, out_bias = (columns.at[n] for n in range(4))
    sums[...] = jnp.zeros_like(sums)
    early[...] = jnp.zeros_like(early)
    late[...] = jnp.zeros_like(late)

    def piece_copy(which, stage, bufs, e):
        peer = lax.rem(crop + e, crops)
        sent, got, _, total = bufs
        src, dst = (sent.at[peer], got.at[crop]) if stage == 0 else (total.at[crop],) * 2
        return pltpu.make_async_remote_copy(
            src_ref=src,
            dst_ref=dst,
            send_sem=sum_sems.at[which, stage, 0, e - 1],
            recv_sem=sum_sems.at[which, stage, 1, e - 1],
            device_id={"dp": peer},
            device_id_type=pl.DeviceIdType.MESH,
        )

    def swap_copy(which, bufs, d):
        part = bufs[2]
        return pltpu.make_async_remote_copy(
            src_ref=part.at[me],
            dst_ref=part.at[me],
            send_sem=swap_sems.at[which, 0, d - 1],
            recv_sem=swap_sems.at[which, 1, d - 1],
            device_id={"dap": lax.rem(me + d, groups)},
            device_id_type=pl.DeviceIdType.MESH,
        )

    piece = channels // crops

    def sum_first(which, acc, bufs):
        for p in range(crops):
            bufs[0][p] = acc[p * piece : (p + 1) * piece, :].astype(bf16)
        for e in range(1, crops):
            piece_copy(which, 0, bufs, e).start()

    def sum_second(which, bufs):
        total = bufs[0][crop].astype(f32)
        for e in range(1, crops):
            piece_copy(which, 0, bufs, e).wait_recv()
            total = total + bufs[1][lax.rem(crop + crops - e, crops)]
        bufs[2][me] = total.astype(bf16)
        for d in range(1, groups):
            swap_copy(which, bufs, d).start()

    def sum_third(which, bufs):
        for d in range(1, groups):
            swap_copy(which, bufs, d).wait_recv()
        total = bufs[2][0].astype(f32)
        for g in range(1, groups):
            total = total + bufs[2][g]
        bufs[3][crop] = (total * (1.0 / length)).astype(bf16)
        for e in range(1, crops):
            piece_copy(which, 1, bufs, e).start()

    def sum_last(which, bufs, outs, stats_out):
        for e in range(1, crops):
            piece_copy(which, 1, bufs, e).wait_recv()
        total = jnp.concatenate([bufs[3][p] for p in range(crops)], axis=0).astype(f32)
        at = 0
        for out in outs:
            out[...] = total[:, at : at + out.shape[1]]
            at += out.shape[1]
        turned_stats = jnp.transpose(total[:, at : at + channels])
        stats_out[0:1, :] = turned_stats[0:1]
        stats_out[1:2, :] = turned_stats[8:9]
        for e in range(1, crops):
            piece_copy(which, 0, bufs, e).wait_send()
            piece_copy(which, 1, bufs, e).wait_send()
        for d in range(1, groups):
            swap_copy(which, bufs, d).wait_send()

    def put_stats(acc, first):
        at = acc.shape[1] - channels
        for n in range(2):
            acc[:, at + 8 * n : at + 8 * n + 8] = jnp.broadcast_to(
                jnp.sum(sums[first + n], axis=1, keepdims=True), (channels, 8)
            )

    def normed_of(x):
        hat, inv = norm_cols(mm_t(eye[...], x))
        return hat, inv, (hat * in_gain[...] + in_bias[...]).astype(bf16)

    def put_part(ref, first, values):
        for r in range(STEP):
            ref[pl.ds(first + r, hidden, stride=cut), :] = values[:, r * length : (r + 1) * length]

    def settle(side, base):
        left_part, right_part = parts[side]

        def body(h, carry):
            frm = pl.ds(pl.multiple_of(h * cut, cut), cut)
            to = pl.ds(pl.multiple_of(h * length + base, cut), cut)
            left[to, :] = left_part[frm, :].astype(bf16)
            right[to, :] = right_part[frm, :].astype(bf16)
            return carry

        lax.fori_loop(0, hidden, body, 0, unroll=8)

    def sides(side, block, c):
        left_part, right_part = parts[side]
        x = cells_of(act_all.at[block], c * STEP)
        _, _, normed = normed_of(x)
        pj = mm(w_t[...], normed)
        first = c % per_cut * STEP
        put_part(left_part, first, sigmoid(pj[0:hidden]) * pj[hidden : 2 * hidden])
        put_part(
            right_part, first, sigmoid(pj[2 * hidden : 3 * hidden]) * pj[3 * hidden : 4 * hidden]
        )
        if c % per_cut == per_cut - 1:
            settle(side, slot_of(block) * rows + c // per_cut * cut)

    def own_sides(c):
        left_part, right_part = parts[0]

        def body(t, carry):
            at = c * (cut // STEP) + t
            x = cells_of(act_all.at[me], at * STEP)
            hat, inv, normed = normed_of(x)
            hat_sc[at] = hat
            inv_sc[at] = inv
            normed_sc[at] = normed
            pj = mm(w_t[...], normed)
            sa, va = sigmoid(pj[0:hidden]), pj[hidden : 2 * hidden]
            sig_a[at] = sa
            rest_a[at] = va * (1.0 - sa)
            put_part(left_part, t * STEP, sa * va)
            sb, vb = sigmoid(pj[2 * hidden : 3 * hidden]), pj[3 * hidden : 4 * hidden]
            sig_b[at] = sb
            rest_b[at] = vb * (1.0 - sb)
            put_part(right_part, t * STEP, sb * vb)
            return carry

        lax.fori_loop(0, cut // STEP, body, 0)
        settle(0, c * cut)

    def own_gate(t, carry):
        gate = sigmoid(mm(wg_t[...], normed_sc[t]))
        cot_t = mm_t(eye[...], cells_of(cot, t * STEP))
        grad = cot_t * gate
        gate_sc[t] = gate
        slope_sc[t] = grad * (1.0 - gate)
        d_mixed = grad.astype(bf16)
        d_mixed_sc[t] = d_mixed
        for r in range(STEP):
            mixed_grad[t * STEP + r] = mm_t(
                eye[...], d_mixed[:, r * length : (r + 1) * length]
            ).astype(bf16)
        d_out = mm(wo[...], d_mixed)
        d_out_sc[t] = d_out
        first_sc[t] = mean_cols(d_out * out_gain[...])
        sums[3] += fold(d_out, length)
        return carry

    def at_end(device):
        return (device == 0) | (device == groups - 1)

    def send_cols(from_end, to_end):
        for q in range(cuts):
            for d in range(1, groups):
                peer_at_end = at_end(lax.rem(me + d, groups))

                @pl.when((at_end(me) == from_end) & (peer_at_end == to_end))
                def _():
                    col_copy(d, q).start()

    act_in.wait()
    for c in range(cuts):
        own_sides(c)
    cot_in.wait()
    lax.fori_loop(0, rows // STEP, own_gate, 0)

    def products(late_half):
        def body(h, carry):
            at = h * length
            half_rows = pl.ds(pl.multiple_of(at + late_half * wide, wide), wide)
            own = pl.ds(pl.multiple_of(at, rows), rows)
            to = pl.ds(pl.multiple_of(h * rows, rows), rows)
            sides_of = [right[half_rows, :], left[half_rows, :]]
            both = mm_t(
                jnp.concatenate([left[own, :], right[own, :]], axis=0),
                jnp.concatenate(sides_of[::-1] if late_half else sides_of, axis=0),
            )
            row_lanes = slice(wide, length) if late_half else slice(0, wide)
            col_lanes = slice(0, wide) if late_half else slice(wide, length)
            tri_r[to, row_lanes] = both[0:rows, row_lanes]
            tri_c[to, col_lanes] = both[rows : 2 * rows, col_lanes]
            return carry

        lax.fori_loop(0, hidden, body, 0, unroll=16)

    for s in range(1, groups):
        low, high = me - s, me + s
        for c in range(hops):

            @pl.when(low >= 0)
            def _():
                hop(act, low, c, right_sem, me).wait_recv()

                @pl.when(me + 1 < groups)
                def _():
                    hop(act_all.at[low], low, c, right_sem, me + 1).start()

            @pl.when(high < groups)
            def _():
                hop(act, high, c, left_sem, me).wait_recv()

                @pl.when(me >= 1)
                def _():
                    hop(act_all.at[high], high, c, left_sem, me - 1).start()

            if s == groups - 1 and c == hops - 1:
                send_cols(True, True)
                send_cols(True, False)
                send_cols(False, False)
                send_cols(False, True)

            @pl.when(low >= 0)
            def _():
                sides(0, low, c)

            @pl.when(high < groups)
            def _():
                sides(1, high, c)

        if s == max(1, groups // 2):
            products(0)

    products(1)

    def slabs(ref, first):
        return jnp.concatenate(
            [ref[pl.ds(first + r, hidden, stride=rows), :] for r in range(STEP)], axis=1
        )

    def put_slabs(ref, first, values):
        for r in range(STEP):
            ref[pl.ds(first + r, hidden, stride=rows), :] = values[
                :, r * length : (r + 1) * length
            ]

    def row_pass(t, carry):
        first = t * STEP
        hat, inv = norm_cols(slabs(tri_r, first).astype(bf16).astype(f32))
        tri_norm = (hat * out_gain[...] + out_bias[...]).astype(bf16)
        d_out = d_out_sc[t]
        scaled = d_out * hat
        sums[2] += fold(scaled, length)
        second = mean_cols(scaled * out_gain[...])
        put_slabs(tri_r, first, (d_out * out_gain[...] - first_sc[t] - hat * second) * inv)
        mixed = mm(wo_t[...], tri_norm)
        update_sc[t] = (gate_sc[t] * mixed).astype(bf16)
        d_gate = (slope_sc[t] * mixed).astype(bf16)
        d_gate_sc[t] = d_gate
        early[:, 0:channels] += mm_t(normed_sc[t], d_gate)
        early[:, channels : 2 * channels] += mm_t(tri_norm, d_mixed_sc[t])
        return carry

    lax.fori_loop(0, rows // STEP, row_pass, 0, unroll=pair)

    def back_rows(h, carry):
        r_all = right[pl.ds(pl.multiple_of(h * length, length), length), :]
        to = pl.ds(pl.multiple_of(h * rows, rows), rows)
        tri_r[to, :] = mm(tri_r[to, :].astype(bf16), r_all)
        return carry

    lax.fori_loop(0, hidden, back_rows, 0, unroll=16)

    half = 2 * hidden

    def half_grad(ref, first, sig, rest):
        d_val = slabs(ref, first).astype(bf16).astype(f32) * sig
        return jnp.concatenate([(d_val * rest).astype(bf16), d_val.astype(bf16)], axis=0)

    def left_pass(t, carry):
        d_proj = half_grad(tri_r, t * STEP, sig_a[t], rest_a[t])
        early[:, 2 * channels : 2 * channels + half] += mm_t(normed_sc[t], d_proj)
        d_normed_sc[t] = mm(w[:, 0:half], d_proj) + mm(wg[...], d_gate_sc[t])
        return carry

    lax.fori_loop(0, rows // STEP, left_pass, 0, unroll=pair)
    put_stats(early, 2)
    sum_first(0, early, early_bufs)

    hat_c, inv_c = d_out_sc, first_sc

    def col_norm(t, carry):
        hat_c[t], inv_c[t] = norm_cols(slabs(tri_c, t * STEP).astype(bf16).astype(f32))
        return carry

    lax.fori_loop(0, rows // STEP, col_norm, 0, unroll=pair)

    def columns_of(ref, first):
        return jnp.concatenate(
            [ref[pl.ds(first + r, length, stride=cut), :] for r in range(STEP)], axis=0
        ).astype(bf16)

    for q in range(cuts):

        def unpack_own(t, carry):
            to = pl.ds(pl.multiple_of((wide + t) * cut, cut), cut)
            col_grad[to, :] = mixed_grad[t, q * cut : q * cut + cut, :].astype(f32)
            return carry

        lax.fori_loop(0, rows, unpack_own, 0, unroll=8)
        for d in range(1, groups):
            col_copy(d, q).wait_recv()
        for d in range(1, groups):
            peer = lax.rem(me + d, groups)

            at = lax.rem(slot_of(peer) * rows + wide, length)

            def unpack_peer(t, carry):
                to = pl.ds(pl.multiple_of((at + t) * cut, cut), cut)
                col_grad[to, :] = mixed_cols[peer * rows + t, q * cut : q * cut + cut, :].astype(f32)
                return carry

            lax.fori_loop(0, rows, unpack_peer, 0, unroll=8)

        def col_pass(t, carry):
            at = q * (cut // STEP) + t
            hat = hat_c[at]
            d_hat = mm_t(wo[...], columns_of(col_grad, t * STEP)) * out_gain[...]
            back = (d_hat - mean_cols(d_hat) - hat * mean_cols(d_hat * hat)) * inv_c[at]
            put_slabs(tri_c, at * STEP, back)
            return carry

        lax.fori_loop(0, cut // STEP, col_pass, 0, unroll=pair_cut)

    sum_second(0, early_bufs)

    def back_cols(h, carry):
        at = h * length
        l_all = jnp.concatenate(
            [left[pl.ds(pl.multiple_of(at + n * wide, wide), wide), :] for n in (1, 0)], axis=0
        )
        to = pl.ds(pl.multiple_of(h * rows, rows), rows)
        tri_c[to, :] = mm(tri_c[to, :].astype(bf16), l_all)
        return carry

    lax.fori_loop(0, hidden, back_cols, 0, unroll=16)
    sum_third(0, early_bufs)

    def right_pass(t, carry):
        d_proj = half_grad(tri_c, t * STEP, sig_b[t], rest_b[t])
        late[:, 0:half] += mm_t(normed_sc[t], d_proj)
        d_normed = mm(w[:, half : 2 * half], d_proj) + d_normed_sc[t]
        sums[0] += fold(d_normed * hat_sc[t], length)
        sums[1] += fold(d_normed, length)
        d_normed_sc[t] = d_normed
        return carry

    lax.fori_loop(0, rows // STEP, right_pass, 0, unroll=pair)
    put_stats(late, 0)
    sum_first(1, late, late_bufs)

    def turn_back(values, out, t):
        for r in range(STEP):
            block = mm_t(eye[...], values[:, r * length : (r + 1) * length]).astype(bf16)
            for n, span in enumerate(spans):
                out[t * STEP + r, span, :] = block[n * rows : (n + 1) * rows]

    def last_pass(t, carry):
        hat = hat_sc[t]
        d_hat = d_normed_sc[t] * in_gain[...]
        back = (d_hat - mean_cols(d_hat) - hat * mean_cols(d_hat * hat)) * inv_sc[t]
        turn_back(back.astype(bf16), pair_grad, t)
        return carry

    def update_pass(t, carry):
        turn_back(update_sc[t], update, t)
        return carry

    lax.fori_loop(0, rows // STEP, last_pass, 0, unroll=pair)
    copy_out(1).start()
    sum_second(1, late_bufs)
    lax.fori_loop(0, rows // STEP, update_pass, 0, unroll=pair)
    copy_out(0).start()
    sum_last(0, early_bufs, (gate_grad, out_grad, proj_grad.at[:, 0:half]), out_norm_grad)
    for n in (3, 4, 6):
        copy_out(n).start()
    sum_third(1, late_bufs)

    for s in range(groups):
        low, high = me - s, me + s

        @pl.when((low >= 0) & (me + 1 < groups))
        def _():
            for c in range(hops):
                hop(act, low, c, right_sem, me + 1).wait_send()

        @pl.when((high < groups) & (me >= 1))
        def _():
            for c in range(hops):
                hop(act, high, c, left_sem, me - 1).wait_send()

    for q in range(cuts):
        for d in range(1, groups):
            col_copy(d, q).wait_send()

    sum_last(1, late_bufs, (proj_grad.at[:, half : 2 * half],), in_norm_grad)
    for n in (2, 5):
        copy_out(n).start()
    for n in range(7):
        copy_out(n).wait()


def finish(count, *refs):
    ins, outs, held, sems = refs[:count], refs[count : 2 * count], refs[2 * count : -1], refs[-1]
    fetch, store = [], []
    for n in range(count):
        parts = PARTS if len(ins[n].shape) == 3 else 1
        size = ins[n].shape[0] // parts
        for p in range(parts):
            part = pl.ds(p * size, size)
            fetch.append(
                pltpu.make_async_copy(ins[n].at[part], held[n].at[part], sems.at[0, n, p])
            )
            store.append(
                pltpu.make_async_copy(held[n].at[part], outs[n].at[part], sems.at[1, n, p])
            )
    for copy in fetch:
        copy.start()
    for arrived, copy in zip(fetch, store):
        arrived.wait()
        copy.start()
    for copy in store:
        copy.wait()


def shards(
    crops,
    groups,
    pair_act,
    pair_cot,
    in_gain,
    in_bias,
    proj_weight,
    gate_weight,
    out_gain,
    out_bias,
    out_weight,
):
    _, rows, length, channels = pair_act.shape
    hidden = out_weight.shape[0]
    act = pair_act.reshape(rows, length, channels)
    cot = pair_cot.reshape(rows, length, channels)
    anywhere = pl.BlockSpec(memory_space=pl.ANY)
    dma = pltpu.SemaphoreType.DMA
    piece = channels // crops
    cut = min(CUT, rows)
    steps, cells = rows // STEP, STEP * length

    def sum_bufs(width):
        return tuple(pltpu.VMEM((n, piece, width), bf16) for n in (crops, crops, groups, crops))

    def per_step(*shape, dtype=f32):
        return pltpu.VMEM((steps, *shape), dtype)

    early_width, late_width = 3 * channels + 2 * hidden, 2 * hidden + channels
    shapes = (
        jax.ShapeDtypeStruct(act.shape, bf16),
        jax.ShapeDtypeStruct(act.shape, bf16),
        jax.ShapeDtypeStruct(proj_weight.shape, f32),
        jax.ShapeDtypeStruct(gate_weight.shape, f32),
        jax.ShapeDtypeStruct(out_weight.shape, f32),
        jax.ShapeDtypeStruct((2, channels), f32),
        jax.ShapeDtypeStruct((2, hidden), f32),
    )
    results = pl.pallas_call(
        functools.partial(kernel, crops, groups),
        out_shape=shapes,
        in_specs=[anywhere] * 9,
        out_specs=(anywhere,) * 7,
        scratch_shapes=[
            pltpu.VMEM((groups, rows, length, channels), bf16),
            pltpu.VMEM((rows, length, channels), bf16),
            pltpu.VMEM((rows, length, channels), bf16),
            pltpu.VMEM((length, rows, channels), bf16),
            pltpu.VMEM((hidden * cut, length), f32),
            pltpu.VMEM((hidden * cut, length), f32),
            pltpu.VMEM((hidden * cut, length), f32),
            pltpu.VMEM((hidden * cut, length), f32),
            pltpu.VMEM((hidden * length, length), bf16),
            pltpu.VMEM((hidden * length, length), bf16),
            pltpu.VMEM((hidden * rows, length), f32),
            pltpu.VMEM((hidden * rows, length), f32),
            pltpu.VMEM((length * cut, channels), f32),
            per_step(channels, cells, dtype=bf16),
            per_step(channels, cells),
            per_step(1, cells),
            per_step(hidden, cells),
            per_step(hidden, cells),
            per_step(hidden, cells),
            per_step(hidden, cells),
            per_step(channels, cells),
            per_step(channels, cells),
            per_step(hidden, cells),
            per_step(1, cells),
            per_step(channels, cells, dtype=bf16),
            per_step(channels, cells, dtype=bf16),
            per_step(channels, cells, dtype=bf16),
            per_step(channels, cells),
            pltpu.VMEM((4, channels, length), f32),
            dma((9,)),
            dma((groups, rows // STEP)),
            dma((groups, rows // STEP)),
            dma((groups, rows // STEP)),
            dma((groups - 1, rows // cut)),
            dma((groups - 1, rows // cut)),
            pltpu.VMEM((4 * hidden, channels), bf16),
            pltpu.VMEM((channels, channels), bf16),
            pltpu.VMEM((channels, hidden), bf16),
            pltpu.VMEM((channels, channels), bf16),
            pltpu.VMEM((4, channels, 1), f32),
            pltpu.VMEM((channels, early_width), f32),
            pltpu.VMEM((channels, late_width), f32),
            sum_bufs(early_width),
            sum_bufs(late_width),
            dma((2, 2, 2, crops - 1)),
            dma((2, 2, groups - 1)),
            *(pltpu.VMEM(shape.shape, shape.dtype) for shape in shapes),
            dma((7,)),
            pltpu.VMEM((1, channels), f32),
            pltpu.VMEM((1, channels), f32),
            pltpu.VMEM(proj_weight.shape, bf16),
            pltpu.VMEM(gate_weight.shape, bf16),
            pltpu.VMEM((1, hidden), f32),
            pltpu.VMEM((1, hidden), f32),
            pltpu.VMEM(out_weight.shape, bf16),
        ],
        compiler_params=pltpu.CompilerParams(
            collective_id=0, has_side_effects=True, vmem_limit_bytes=60 * 1024 * 1024
        ),
        name="tri",
    )(
        act,
        cot,
        in_gain.reshape(1, channels),
        in_bias.reshape(1, channels),
        proj_weight,
        gate_weight,
        out_gain.reshape(1, hidden),
        out_bias.reshape(1, hidden),
        out_weight,
    )
    update, pair_grad, *grads = pl.pallas_call(
        functools.partial(finish, 7),
        out_shape=shapes,
        in_specs=[anywhere] * 7,
        out_specs=(anywhere,) * 7,
        scratch_shapes=[*(pltpu.VMEM(shape.shape, shape.dtype) for shape in shapes), dma((2, 7, PARTS))],
        name="finish",
    )(*results)
    return (update.reshape(pair_act.shape), pair_grad.reshape(pair_act.shape), *grads)


def solution(mesh):
    placed = (P("dp", "dap", None, None),) * 2 + (P(),) * 7
    return jax.shard_map(
        functools.partial(shards, mesh.shape["dp"], mesh.shape["dap"]),
        mesh=mesh,
        in_specs=placed,
        out_specs=(P("dp", "dap", None, None), P("dp", "dap", None, None), P(), P(), P(), P(), P()),
        check_vma=False,
    )
```
